256 devices in a mesh: dp: 4 (over y), ctx: 64 (over z, x, core).
Axes of the slice: x: 4, y: 4, z: 8, core: 2. Of those that a mesh axis runs over, the one named last changes fastest.
Arguments:
- projected: bfloat16 [4, 8192, 12288], P('dp', 'ctx'), may hold values from -6 to 6
- doc_ids: int32 [4, 8192], P('dp'), may hold values from 0 to 15, never falling along the last dimension, each value on 1 to 1024 neighbouring positions
- short_filter: float32 [3, 12288], replicated, may hold values from -3.5 to 3.5
- long_filter: bfloat16 [256, 128], replicated, may hold values from -0.5 to 0.5
- cotangent: bfloat16 [4, 8192, 4096], P('dp', 'ctx'), may hold values from -6 to 6
Outputs:
- block_out: bfloat16 [4, 8192, 4096], P('dp', 'ctx')
- grad_projected: bfloat16 [4, 8192, 12288], P('dp', 'ctx')
- grad_short: float32 [3, 12288], P(None, 'ctx')
- grad_long: float32 [256, 128], P('ctx')
The draws below stay inside these ranges and needn't reach their ends.
Inputs may be any that keep to these rules, and one draw needn't show every extreme that they name: `doc_ids`: document numbers never fall along a row, each document spans 1 to 1024 positions, and some document spans exactly 1024.
All inputs are finite; a program needn't handle non-finite values.
Results may differ from the reference program's by a relative error of at most 0.0076.
Values may be sent and summed in bfloat16 or wider, within the bound.
A program may use at most 256 MiB of HBM per device.

```python
import math
import jax
import jax.numpy as jnp
import numpy as np
from jax import lax

D = 4096
SHORT_TAPS = 3
MED_TAPS = 128
DOCS = 16
GROUPS = 256
WINDOW = 8192
DOC_MOST = 1024
BATCH = 4
N_DP = 4


def levels(stream_key, shape, cuts, smallest, high):
    def one(position, parts):
        steps = jax.random.uniform(jax.random.fold_in(jax.random.fold_in(stream_key, 6), position), (parts,), jnp.float32, smallest / len(cuts), high / len(cuts))
        return jnp.repeat(jnp.exp(steps), shape[position] // parts).reshape((-1,) + (1,) * (len(shape) - position - 1))

    level = one(*cuts[0])
    for cut in cuts[1:]:
        level = level * one(*cut)
    return level


def profile(count, total, limit, skew):
    portions = [(1 << 20) // math.isqrt(standing ** skew) + 1 for standing in range(2, count + 1)]
    surplus, given = total - limit - (count - 1), [1] * (count - 1)
    while surplus > 0:
        free = [i for i in range(count - 1) if given[i] < limit]
        mass, left = sum([portions[i] for i in free]), surplus
        for i in free:
            more = min(limit - given[i], max(1, left * portions[i] // mass), surplus)
            given[i] = given[i] + more
            surplus = surplus - more
    return np.array([limit] + given)


def uneven_parts(own_key, amount, total, reach, lean):
    if amount == 2:
        one = jax.random.randint(own_key, (), max(1, total - reach), min(reach, total - 1) + 1)
        return jnp.stack([one, total - one])
    tallies = jnp.asarray(profile(amount, total, reach, lean), jnp.int32)
    twos = (amount - 1) // 2
    giver, taker = tallies[1:1 + 2 * twos:2], tallies[2:2 + 2 * twos:2]
    margin = jnp.minimum(giver - 1, reach - taker)
    passed = jax.random.randint(jax.random.fold_in(own_key, 1), (twos,), 0, 1 << 20) % (margin + 1)
    tallies = tallies.at[1:1 + 2 * twos:2].set(giver - passed).at[2:2 + 2 * twos:2].set(taker + passed)
    return tallies[jax.random.permutation(jax.random.fold_in(own_key, 2), amount)]


def normal_values(stream_key, shape, deviation, reach, shards=(), kind=jnp.bfloat16):
    drawn = deviation * jax.random.normal(stream_key, shape, jnp.float32)
    if shards:
        drawn = drawn * levels(stream_key, shape, shards, -0.22, 0.18)
    return jnp.clip(drawn, -reach, reach).astype(kind)


def setup_inputs(seed: int = 0) -> dict:
    keys = jax.random.split(jax.random.key(seed), 6)
    projected = normal_values(keys[0], (BATCH, WINDOW, 3 * D), 1.0, 6.0, ((0, 4), (1, 64)))
    doc_ids = jax.vmap(lambda own: jnp.searchsorted(jnp.cumsum(uneven_parts(own, DOCS, WINDOW, DOC_MOST, 2)), jnp.arange(WINDOW), side="right"))(jax.random.split(keys[1], BATCH)).reshape((BATCH, WINDOW)).astype(jnp.int32)
    short_filter = normal_values(keys[2], (SHORT_TAPS, 3 * D), SHORT_TAPS ** -0.5, 3.5, (), jnp.float32)
    long_filter = normal_values(keys[3], (GROUPS, MED_TAPS), MED_TAPS ** -0.5, 0.5)
    cotangent = normal_values(keys[4], (BATCH, WINDOW, D), 1.0, 6.0, ((0, 4), (1, 64)))
    return dict(projected=projected, doc_ids=doc_ids, short_filter=short_filter, long_filter=long_filter, cotangent=cotangent)


def doc_offsets(seg_row):
    length = seg_row.shape[0]
    places = jnp.arange(length, dtype=jnp.int32)
    starts_here = jnp.concatenate([jnp.ones((1,), bool), seg_row[1:] != seg_row[:-1]])
    return (places - lax.cummax(jnp.where(starts_here, places, 0), axis=0)).astype(jnp.int32)

def toeplitz(filters):
    groups, tap_count = filters.shape
    widened = jnp.concatenate([jnp.zeros((groups, tap_count), filters.dtype), filters[:, ::-1], jnp.zeros((groups, tap_count - 1), filters.dtype)], axis=1)
    tiled_rows = jnp.tile(widened, (1, tap_count))
    span_len = 3 * tap_count - 2
    return tiled_rows[:, tap_count - 1:tap_count - 1 + tap_count * span_len].reshape(groups, tap_count, span_len)[:, :, :2 * tap_count]

def short_forward(extended, weights, offsets):
    short_taps = weights.shape[0]
    tok_count = offsets.shape[0]
    running = jnp.zeros((tok_count, extended.shape[1]), jnp.float32)
    for tap_pos in range(short_taps):
        shifted = extended[short_taps - 1 - tap_pos:short_taps - 1 - tap_pos + tok_count].astype(jnp.float32)
        running = running + jnp.where((offsets >= tap_pos)[:, None], weights[tap_pos][None, :] * shifted, 0.0)
    return running

def short_backward(grads_ext, offsets_ext, extended, weights, offsets):
    short_taps = weights.shape[0]
    tok_count = offsets.shape[0]
    running = jnp.zeros((tok_count, extended.shape[1]), jnp.float32)
    pieces = []
    for tap_pos in range(short_taps):
        ahead_part = grads_ext[tap_pos:tap_pos + tok_count].astype(jnp.float32)
        keep_mask = (offsets_ext[tap_pos:tap_pos + tok_count] >= tap_pos)[:, None]
        running = running + jnp.where(keep_mask, weights[tap_pos][None, :] * ahead_part, 0.0)
        shifted = extended[short_taps - 1 - tap_pos:short_taps - 1 - tap_pos + tok_count].astype(jnp.float32)
        local_grad = grads_ext[:tok_count].astype(jnp.float32)
        pieces.append(lax.optimization_barrier(jnp.sum(jnp.where((offsets >= tap_pos)[:, None], local_grad * shifted, 0.0), axis=0)))
    return (running, jnp.stack(pieces, axis=0))

def reference(projected, doc_ids, short_filter, long_filter, cotangent):
    kernel = toeplitz(long_filter).astype(jnp.float32)
    groups, tap_count = long_filter.shape
    model_width = cotangent.shape[2]
    length = projected.shape[1]
    blocks = length // tap_count
    short_taps = short_filter.shape[0]
    row_ids = jnp.arange(tap_count, dtype=jnp.int32)[:, None]
    col_ids = jnp.arange(2 * tap_count, dtype=jnp.int32)[None, :]

    def one_window(window_items):
        inputs_row, seg_row, grad_row = window_items
        offsets = doc_offsets(seg_row)
        extended = jnp.concatenate([jnp.zeros((short_taps - 1, inputs_row.shape[1]), jnp.bfloat16), inputs_row], axis=0)
        mixed_in = short_forward(extended, short_filter, offsets).astype(jnp.bfloat16)
        queries = mixed_in[:, :model_width]
        key_part = mixed_in[:, model_width:2 * model_width]
        value_part = mixed_in[:, 2 * model_width:]
        product = (key_part.astype(jnp.float32) * value_part.astype(jnp.float32)).astype(jnp.bfloat16)
        grad_mix = (grad_row.astype(jnp.float32) * queries.astype(jnp.float32)).astype(jnp.bfloat16)
        source = jnp.concatenate([jnp.zeros((tap_count, model_width), jnp.bfloat16), product], axis=0)

        def block_step(state_pair, block_id):
            spread_acc, kernel_grad = state_pair
            first_row = block_id * tap_count
            window = lax.dynamic_slice_in_dim(source, first_row, 2 * tap_count, 0).astype(jnp.float32).reshape(2 * tap_count, groups, -1)
            near_offs = lax.dynamic_slice_in_dim(offsets, first_row, tap_count, 0)
            keep_mask = row_ids + tap_count - col_ids <= near_offs[:, None]
            masked = jnp.where(keep_mask[None], kernel, 0.0)
            grad_block = lax.dynamic_slice_in_dim(grad_mix, first_row, tap_count, 0).astype(jnp.float32).reshape(tap_count, groups, -1)
            mixed_block = jnp.einsum('gis,sgc->igc', masked, window, precision=lax.Precision.HIGHEST)
            spread = jnp.einsum('gis,igc->sgc', masked, grad_block, precision=lax.Precision.HIGHEST)
            inner_prod = jnp.einsum('igc,sgc->gis', grad_block, window, precision=lax.Precision.HIGHEST)
            kernel_grad = kernel_grad + jnp.where(keep_mask[None], inner_prod, 0.0)
            old_part = lax.dynamic_slice_in_dim(spread_acc, first_row, 2 * tap_count, 0)
            spread_acc = lax.dynamic_update_slice_in_dim(spread_acc, old_part + spread.reshape(2 * tap_count, model_width), first_row, 0)
            return ((spread_acc, kernel_grad), mixed_block.reshape(tap_count, model_width))
        init_state = (jnp.zeros((length + tap_count, model_width), jnp.float32), jnp.zeros((groups, tap_count, 2 * tap_count), jnp.float32))
        (spread_acc, kernel_grad), mixed_blocks = lax.scan(block_step, init_state, jnp.arange(blocks, dtype=jnp.int32))
        long_mix = mixed_blocks.reshape(length, model_width).astype(jnp.bfloat16)
        grad_product = spread_acc[tap_count:].astype(jnp.float32).astype(jnp.bfloat16)
        block_out = (queries.astype(jnp.float32) * long_mix.astype(jnp.float32)).astype(jnp.bfloat16)
        grad_queries = (grad_row.astype(jnp.float32) * long_mix.astype(jnp.float32)).astype(jnp.bfloat16)
        grad_keys = (grad_product.astype(jnp.float32) * value_part.astype(jnp.float32)).astype(jnp.bfloat16)
        grad_values = (grad_product.astype(jnp.float32) * key_part.astype(jnp.float32)).astype(jnp.bfloat16)
        mixed_grad = jnp.concatenate([grad_queries, grad_keys, grad_values], axis=1)
        grads_ext = jnp.concatenate([mixed_grad, jnp.zeros((short_taps - 1, mixed_grad.shape[1]), jnp.bfloat16)], axis=0)
        offsets_ext = jnp.concatenate([offsets, jnp.zeros((short_taps - 1,), jnp.int32)], axis=0)
        grad_inputs, weight_grad = short_backward(grads_ext, offsets_ext, extended, short_filter, offsets)
        return (block_out, grad_inputs.astype(jnp.bfloat16), weight_grad, kernel_grad)
    block_out, grad_projected, weight_grads, kernel_grads = lax.map(one_window, (projected, doc_ids, cotangent))
    norm_scale = N_DP * length
    grad_short = lax.optimization_barrier(jnp.sum(weight_grads, axis=0)) / math.sqrt(norm_scale)
    _, pull_back = jax.vjp(toeplitz, long_filter.astype(jnp.float32))
    group_size = model_width // groups
    grad_long = pull_back(lax.optimization_barrier(jnp.sum(kernel_grads, axis=0)))[0] / math.sqrt(norm_scale * group_size)
    return (block_out, grad_projected, grad_short, grad_long)
```

```python
import functools
import math

import jax
import jax.numpy as jnp
from jax import lax
from jax.experimental import pallas as pl
from jax.experimental.pallas import tpu as pltpu
from jax.sharding import PartitionSpec as P

BF = jnp.bfloat16
F32 = jnp.float32
ROWS = 32
LANES = 128


def passed_along(value, axis, steps):
    count = lax.axis_size(axis)
    first, last = (max(0, -steps), min(count, count - steps))
    return lax.ppermute(value, axis, [(s, s + steps) for s in range(first, last)])


def same(cols, other):
    return cols[:, 0:1] == cols[:, other : other + 1]


def mix_kernel(cols_ref, q_ref, k_ref, v_ref, bq_ref, bk_ref, bv_ref, wq_ref, wk_ref, wv_ref, cot_ref,
               q_out, k_out, v_out, prod_ref, gm_ref, ext):
    cols = cols_ref[...]
    tok = q_ref.shape[0]
    one, two = same(cols, 1), same(cols, 2)

    def mixed(x_ref, b_ref, w_ref, out):
        x = x_ref[...].astype(F32)
        ext[6:8, :] = b_ref[...].astype(F32)
        ext[8 : 8 + tok, :] = x
        total = w_ref[0:1, :] * x
        total = total + jnp.where(one, w_ref[1:2, :] * ext[7 : 7 + tok, :], 0.0)
        total = total + jnp.where(two, w_ref[2:3, :] * ext[6 : 6 + tok, :], 0.0)
        rounded = total.astype(BF)
        out[...] = rounded
        return rounded.astype(F32)

    gm_ref[...] = (cot_ref[...].astype(F32) * mixed(q_ref, bq_ref, wq_ref, q_out)).astype(BF)
    key = mixed(k_ref, bk_ref, wk_ref, k_out)
    prod_ref[...] = (key * mixed(v_ref, bv_ref, wv_ref, v_out)).astype(BF)


def banded(filters, rows):
    parts = []
    for g in range(filters.shape[0]):
        wide = jnp.broadcast_to(filters[g : g + 1, :], (rows, filters.shape[1]))
        parts.append(pltpu.roll(wide, 0, 1, stride=1, stride_axis=0))
    return jnp.concatenate(parts, axis=0).astype(BF)


def window(first, second, start, size):
    tok = first.shape[0]
    if start + size <= tok:
        return first[start : start + size]
    return jnp.concatenate([first[start:], second[: start + size - tok]], axis=0)


def long_kernel(groups, cols_ref, dwin_ref, filt_ref, q_ref, k_ref, v_ref, cot_ref, prod_ref, gm_ref,
                before_ref, after_ref, out_ref, mg_ref, gl_ref):
    rows = ROWS
    tok, width = q_ref.shape
    steps = tok // rows
    reach = rows + tok
    lane_group = lax.broadcasted_iota(jnp.int32, (rows, LANES), 1) // (LANES // groups)
    docs = cols_ref[:, 0:1]
    masks = [docs[(a % steps) * rows : (a % steps + 1) * rows] == dwin_ref[a : a + 1, :] for a in range(2 * steps)]
    masks = [jnp.where(m, 1.0, 0.0) for m in masks]

    def block(i, carry):
        at = pl.ds(pl.multiple_of(i * LANES, LANES), LANES)
        filt = filt_ref[pl.ds(pl.multiple_of(i * groups, groups), groups), :]
        prod, gm = prod_ref[:, at], gm_ref[:, at]
        before, after = before_ref[:, at], after_ref[:, at]

        def pick(value):
            total = value[:rows]
            for g in range(1, groups):
                total = jnp.where(lane_group == g, value[g * rows : (g + 1) * rows], total)
            return total

        ahead = banded(filt[:, : 2 * tok], rows)
        back = banded(filt[:, 2 * tok :], rows)
        diag = jnp.zeros((groups * rows, reach), F32)
        for a in range(steps):
            here = slice(a * rows, (a + 1) * rows)
            keep = jnp.concatenate([masks[a].astype(BF)] * groups, axis=0)
            mix = jnp.dot((ahead * keep)[:, :reach], window(before, prod, a * rows, reach), preferred_element_type=F32)
            mix = pick(mix).astype(BF).astype(F32)
            out_ref[here, at] = (q_ref[here, at].astype(F32) * mix).astype(BF)
            mg_ref[0, here, at] = (cot_ref[here, at].astype(F32) * mix).astype(BF)
            keep32 = jnp.concatenate([masks[steps + a]] * groups, axis=0)
            span = window(gm, after, a * rows, reach)
            gp = jnp.dot((back * keep32.astype(BF))[:, :reach], span, preferred_element_type=F32)
            gp = pick(gp).astype(BF).astype(F32)
            mg_ref[1, here, at] = (gp * v_ref[here, at].astype(F32)).astype(BF)
            mg_ref[2, here, at] = (gp * k_ref[here, at].astype(F32)).astype(BF)
            mine = prod[here]
            spread = jnp.concatenate([jnp.where(lane_group == g, mine, jnp.zeros_like(mine)) for g in range(groups)], axis=0)
            pairs = lax.dot_general(spread, span, (((1,), (1,)), ((), ())), preferred_element_type=F32)
            diag = diag + pairs * keep32[:, :reach]
        diag = jnp.concatenate([diag, jnp.zeros((groups * rows, 2 * tok - reach), F32)], axis=1)
        fold = diag.reshape(groups, rows, 2 * tok)
        half = rows // 2
        while half >= 8:
            fold = fold[:, :half] + pltpu.roll(fold[:, half:], 2 * tok - half, 2)
            half //= 2
        while half >= 1:
            fold = fold + pltpu.roll(pltpu.roll(fold, 8 - half, 1), 2 * tok - half, 2)
            half //= 2
        gl_ref[pl.ds(pl.multiple_of(i * groups, groups), groups), :] = fold[:, 0, :tok]
        return carry

    lax.fori_loop(0, width // LANES, block, 0)


def close_kernel(cols_ref, mg_ref, next_ref, x_ref, b_ref, w_ref, out_ref, gs_ref, ext, grad):
    cols = cols_ref[...]
    tok = x_ref.shape[0]
    g = mg_ref[0].astype(F32)
    grad[0:tok, :] = g
    grad[tok : tok + 2, :] = next_ref[0].astype(F32)
    x = x_ref[...].astype(F32)
    ext[6:8, :] = b_ref[...].astype(F32)
    ext[8 : 8 + tok, :] = x
    total = w_ref[0:1, :] * g
    total = total + jnp.where(same(cols, 3), w_ref[1:2, :] * grad[1 : 1 + tok, :], 0.0)
    total = total + jnp.where(same(cols, 4), w_ref[2:3, :] * grad[2 : 2 + tok, :], 0.0)
    out_ref[...] = total.astype(BF)
    gs_ref[0:1, :] = jnp.sum(g * x, axis=0, keepdims=True)
    gs_ref[1:2, :] = jnp.sum(jnp.where(same(cols, 1), g * ext[7 : 7 + tok, :], 0.0), axis=0, keepdims=True)
    gs_ref[2:3, :] = jnp.sum(jnp.where(same(cols, 2), g * ext[6 : 6 + tok, :], 0.0), axis=0, keepdims=True)


def tables(doc_row, first, tok):
    span = 4 * tok
    padded = jnp.concatenate([jnp.full((tok,), -1, jnp.int32), doc_row, jnp.full((2 * tok,), -2, jnp.int32)])
    near = lax.dynamic_slice_in_dim(padded, first, span, 0)
    cols = jnp.stack([near[tok + d : 2 * tok + d] for d in (0, -1, -2, 1, 2, 0, 0, 0)], axis=1)
    dwin = jnp.stack([near[a * ROWS : a * ROWS + 2 * tok] for a in range(2 * tok // ROWS)], axis=0)
    return cols, dwin


def wide_filters(long_filter):
    taps = long_filter.shape[1]
    f = long_filter.astype(F32)
    return jnp.concatenate(
        [jnp.pad(f[:, ::-1], ((0, 0), (1, taps - 1))), jnp.pad(f, ((0, 0), (0, taps)))], axis=1
    )


def mix_call(cols, x, border, w, cot, chunk):
    tok, width = cot.shape
    n = width // chunk
    third = [lambda i, p=p: (0, p * n + i) for p in range(3)]
    flat = lambda i: (0, i)
    shape = jax.ShapeDtypeStruct((tok, width), BF)
    return pl.pallas_call(
        mix_kernel,
        grid=(n,),
        out_shape=[shape] * 5,
        in_specs=[pl.BlockSpec((tok, 8), lambda i: (0, 0))]
        + [pl.BlockSpec((tok, chunk), m) for m in third]
        + [pl.BlockSpec((2, chunk), m) for m in third]
        + [pl.BlockSpec((3, chunk), m) for m in third]
        + [pl.BlockSpec((tok, chunk), flat)],
        out_specs=[pl.BlockSpec((tok, chunk), flat)] * 5,
        scratch_shapes=[pltpu.VMEM((8 + tok, chunk), F32)],
        compiler_params=pltpu.CompilerParams(vmem_limit_bytes=48 << 20),
        name="mix",
    )(cols, x, x, x, border, border, border, w, w, w, cot)


def long_call(cols, dwin, filt, q, k, v, cot, prod, gm, before, after, groups_total, chunk):
    tok, width = cot.shape
    per = width // groups_total
    n = width // chunk
    flat = pl.BlockSpec((tok, chunk), lambda i: (0, i))
    return pl.pallas_call(
        functools.partial(long_kernel, LANES // per),
        grid=(n,),
        out_shape=[
            jax.ShapeDtypeStruct((tok, width), BF),
            jax.ShapeDtypeStruct((3, tok, width), BF),
            jax.ShapeDtypeStruct((groups_total, tok), F32),
        ],
        in_specs=[
            pl.BlockSpec((tok, 8), lambda i: (0, 0)),
            pl.BlockSpec(dwin.shape, lambda i: (0, 0)),
            pl.BlockSpec((chunk // per, 4 * tok), lambda i: (i, 0)),
        ]
        + [flat] * 8,
        out_specs=[
            flat,
            pl.BlockSpec((3, tok, chunk), lambda i: (0, 0, i)),
            pl.BlockSpec((chunk // per, tok), lambda i: (i, 0)),
        ],
        compiler_params=pltpu.CompilerParams(vmem_limit_bytes=48 << 20),
        name="long",
    )(cols, dwin, filt, q, k, v, cot, prod, gm, before, after)


def close_call(cols, mg, ahead, x, border, w, chunk):
    tok, width = x.shape
    n = mg.shape[2] // chunk
    third = lambda p, i: (0, p * n + i)
    return pl.pallas_call(
        close_kernel,
        grid=(3, n),
        out_shape=[jax.ShapeDtypeStruct((tok, width), BF), jax.ShapeDtypeStruct((3, width), F32)],
        in_specs=[
            pl.BlockSpec((tok, 8), lambda p, i: (0, 0)),
            pl.BlockSpec((1, tok, chunk), lambda p, i: (p, 0, i)),
            pl.BlockSpec((1, 2, chunk), lambda p, i: (p, 0, i)),
            pl.BlockSpec((tok, chunk), third),
            pl.BlockSpec((2, chunk), third),
            pl.BlockSpec((3, chunk), third),
        ],
        out_specs=[pl.BlockSpec((tok, chunk), third), pl.BlockSpec((3, chunk), third)],
        scratch_shapes=[pltpu.VMEM((8 + tok, chunk), F32), pltpu.VMEM((8 + tok, chunk), F32)],
        compiler_params=pltpu.CompilerParams(vmem_limit_bytes=48 << 20),
        name="close",
    )(cols, mg, ahead, x, border, w)


def local(projected, doc_ids, short_filter, long_filter, cotangent):
    x, cot = projected[0], cotangent[0]
    tok, width = cot.shape
    groups, taps = long_filter.shape
    parts = lax.axis_size("ctx")
    cols, dwin = tables(doc_ids[0], lax.axis_index("ctx") * tok, tok)
    border = passed_along(x[tok - 2 :], "ctx", 1)
    q, k, v, prod, gm = mix_call(cols, x, border, short_filter, cot, 512)
    before = passed_along(prod, "ctx", 1)
    after = passed_along(gm, "ctx", -1)
    out, mg, gl = long_call(
        cols, dwin, wide_filters(long_filter), q, k, v, cot, prod, gm, before, after, groups, 512
    )
    ahead = passed_along(mg[:, :2], "ctx", -1)
    gx, gs = close_call(cols, mg, ahead, x, border, short_filter, 512)
    own_s, own_l = gs.shape[1] // parts, groups // parts
    packed = jnp.concatenate(
        [gs.reshape(3, parts, own_s).transpose(1, 0, 2).reshape(parts, -1), gl.reshape(parts, -1)], axis=1
    )
    total = lax.psum(lax.psum_scatter(packed, "ctx", scatter_dimension=0, tiled=True), "dp")[0]
    norm = lax.axis_size("dp") * doc_ids.shape[1]
    grad_short = total[: 3 * own_s].reshape(3, own_s) / math.sqrt(norm)
    grad_long = total[3 * own_s :].reshape(own_l, taps) / math.sqrt(norm * (width // groups))
    return out[None], gx[None], grad_short, grad_long


def solution(mesh):
    return jax.shard_map(
        local,
        mesh=mesh,
        in_specs=(P("dp", "ctx", None), P("dp", None), P(), P(), P("dp", "ctx", None)),
        out_specs=(P("dp", "ctx", None), P("dp", "ctx", None), P(None, "ctx"), P("ctx", None)),
        check_vma=False,
    )
```

```python
import functools
import math

import jax
import jax.numpy as jnp
from jax import lax
from jax.experimental import pallas as pl
from jax.experimental.pallas import tpu as pltpu
from jax.sharding import PartitionSpec as P

BF = jnp.bfloat16
F32 = jnp.float32
MESH = pl.DeviceIdType.MESH
ROWS = 16
LANES = 128
CORES = 2
ACROSS = 4
VMEM = 56 << 20


def passed_along(value, axis, steps):
    count = lax.axis_size(axis)
    first, last = (max(0, -steps), min(count, count - steps))
    return lax.ppermute(value, axis, [(s, s + steps) for s in range(first, last)])


def near_docs(doc_ref, tok):
    me = lax.axis_index("ctx")
    last = lax.axis_size("ctx") - 1
    at = lambda i: doc_ref[:, pl.ds(pl.multiple_of(i * tok, tok), tok)]
    before = jnp.where(me > 0, at(jnp.maximum(me - 1, 0)), -1)
    after = jnp.where(me < last, at(jnp.minimum(me + 1, last)), -2)
    return jnp.concatenate([before, at(me), after], axis=1).astype(F32)


def doc_column(row):
    return jnp.broadcast_to(row, (row.shape[1], row.shape[1])).T


def shift_matrix(col, row, steps):
    size = col.shape[0]
    place = lax.broadcasted_iota(jnp.int32, (size, size), 1) - lax.broadcasted_iota(jnp.int32, (size, size), 0)
    return jnp.where((place == steps) & (col == row), 1.0, 0.0).astype(BF)


def mix_kernel(doc_ref, q_ref, k_ref, v_ref, bq_ref, bk_ref, bv_ref, wq_ref, wk_ref, wv_ref, cot_ref,
               q_out, k_out, v_out, prod_ref, gm_ref, shifts, edge):
    tok, chunk = q_ref.shape
    wide = 2 * LANES

    @pl.when(pl.program_id(0) == 0)
    def _():
        docs = near_docs(doc_ref, tok)
        own = docs[:, tok : 2 * tok]
        col = doc_column(own)
        shifts[0:tok, :] = shift_matrix(col, own, -1)
        shifts[tok:, :] = shift_matrix(col, own, -2)
        place = lax.broadcasted_iota(jnp.int32, (8, LANES), 0)
        old = [jnp.broadcast_to(docs[:, tok - d : tok - d + 1], (8, LANES)) for d in (1, 2)]
        first = col[:8, :]
        edge[0] = jnp.where((place == 0) & (first == old[0]), 1.0, 0.0)
        edge[1] = jnp.where((place == 0) & (first == old[1]), 1.0, 0.0)
        edge[2] = jnp.where((place == 1) & (first == old[0]), 1.0, 0.0)

    edges = [jnp.concatenate([edge[i]] * 2, axis=1) for i in range(3)]

    def mixed(x_ref, b_ref, w_ref, out, at):
        x = x_ref[:, at]
        moved = jnp.dot(shifts[...], x, preferred_element_type=F32)
        border = b_ref[:, at].astype(F32)
        w = w_ref[:, at]
        total = w[0:1] * x.astype(F32) + w[1:2] * moved[:tok] + w[2:3] * moved[tok:]
        fix = w[1:2] * (edges[0] * border[1:2]) + w[2:3] * (edges[1] * border[0:1] + edges[2] * border[1:2])
        total = jnp.concatenate([total[:8] + fix, total[8:]], axis=0)
        rounded = total.astype(BF)
        out[:, at] = rounded
        return rounded.astype(F32)

    for i in range(chunk // wide):
        at = slice(i * wide, (i + 1) * wide)
        gm_ref[:, at] = (cot_ref[:, at].astype(F32) * mixed(q_ref, bq_ref, wq_ref, q_out, at)).astype(BF)
        key = mixed(k_ref, bk_ref, wk_ref, k_out, at)
        prod_ref[:, at] = (key * mixed(v_ref, bv_ref, wv_ref, v_out, at)).astype(BF)


def banded(filt, rows):
    parts = []
    for g in range(filt.shape[0]):
        wide = jnp.broadcast_to(filt[g : g + 1, :], (rows, filt.shape[1]))
        parts.append(pltpu.roll(wide, 0, 1, stride=1, stride_axis=0).astype(BF))
    return parts


def diagonal_sums(part, width):
    half = part.shape[0] // 2
    while half >= 8:
        part = part[:half] + pltpu.roll(part[half:], width - half, 1)
        half //= 2
    while half >= 1:
        part = part + pltpu.roll(pltpu.roll(part, 8 - half, 0), width - half, 1)
        half //= 2
    return part[0:1]


def long_kernel(groups, doc_ref, filt_ref, q_ref, k_ref, v_ref, cot_ref, prod_ref, gm_ref,
                before_ref, after_ref, out_ref, mg_ref, gl_ref, keeps, keeps32, pwin, gwin, wide):
    rows = ROWS
    tok, width = q_ref.shape
    steps = tok // rows
    lane_group = lax.broadcasted_iota(jnp.int32, (rows, LANES), 1) // (LANES // groups)

    @pl.when(pl.program_id(0) == 0)
    def _():
        docs = near_docs(doc_ref, tok)
        col = doc_column(docs[:, tok : 2 * tok])
        col = jnp.concatenate([col, col], axis=1)
        row = jnp.concatenate([jnp.broadcast_to(docs, (8, 3 * tok)), jnp.full((8, tok), -3.0, F32)], axis=1)
        for a in range(steps):
            mine = col[a * rows : (a + 1) * rows]
            for b, start in ((a, a * rows), (steps + a, tok + a * rows)):
                window = pltpu.roll(row, (4 * tok - start) % (4 * tok), 1)[0:1, : 2 * tok]
                keep = jnp.where(mine == window, 1.0, 0.0)
                keeps32[b * rows : (b + 1) * rows, :] = keep
                keeps[b * rows : (b + 1) * rows, :] = keep.astype(BF)
        pwin[2 * tok :, :] = jnp.zeros((tok, width), BF)
        gwin[2 * tok :, :] = jnp.zeros((tok, width), BF)

    pwin[0:tok, :] = before_ref[...]
    pwin[tok : 2 * tok, :] = prod_ref[...]
    gwin[0:tok, :] = gm_ref[...]
    gwin[tok : 2 * tok, :] = after_ref[...]
    filt = filt_ref[...]
    total = filt.shape[0]
    turn = lax.broadcasted_iota(jnp.int32, (tok, tok), 0) + lax.broadcasted_iota(jnp.int32, (tok, tok), 1)
    turned = jnp.dot(filt, jnp.where(turn == tok, 1.0, 0.0).astype(BF), preferred_element_type=F32)
    filt = filt.astype(F32)
    lane = lax.broadcasted_iota(jnp.int32, (total, tok), 1)
    wide[:, 0:tok] = turned
    wide[:, tok : 2 * tok] = jnp.where(lane == 0, filt, 0.0)
    wide[:, 2 * tok : 3 * tok] = filt
    wide[:, 3 * tok :] = jnp.zeros((total, tok), F32)

    def pick(value):
        chosen = value[:rows]
        for g in range(1, groups):
            chosen = jnp.where(lane_group == g, value[g * rows : (g + 1) * rows], chosen)
        return chosen

    for i in range(width // LANES):
        at = slice(i * LANES, (i + 1) * LANES)
        own = slice(i * groups, (i + 1) * groups)
        ahead = banded(wide[own, : 2 * tok], rows)
        back = banded(wide[own, 2 * tok :], rows)
        diag = None
        for a in range(steps):
            here = slice(a * rows, (a + 1) * rows)
            there = slice((steps + a) * rows, (steps + a + 1) * rows)
            span = slice(a * rows, a * rows + 2 * tok)
            keep = keeps[here, :]
            mix = jnp.dot(jnp.concatenate([b * keep for b in ahead], axis=0), pwin[span, at], preferred_element_type=F32)
            mix = pick(mix).astype(BF).astype(F32)
            out_ref[here, at] = (q_ref[here, at].astype(F32) * mix).astype(BF)
            mg_ref[0, here, at] = (cot_ref[here, at].astype(F32) * mix).astype(BF)
            keep = keeps[there, :]
            grad = jnp.dot(jnp.concatenate([b * keep for b in back], axis=0), gwin[span, at], preferred_element_type=F32)
            grad = pick(grad).astype(BF).astype(F32)
            mg_ref[1, here, at] = (grad * v_ref[here, at].astype(F32)).astype(BF)
            mg_ref[2, here, at] = (grad * k_ref[here, at].astype(F32)).astype(BF)
            mine = prod_ref[here, at]
            zero = jnp.zeros_like(mine)
            spread = jnp.concatenate([jnp.where(lane_group == g, mine, zero) for g in range(groups)], axis=0)
            pairs = lax.dot_general(spread, gwin[span, at], (((1,), (1,)), ((), ())), preferred_element_type=F32)
            keep = keeps32[there, :]
            pairs = [pairs[g * rows : (g + 1) * rows] * keep for g in range(groups)]
            diag = pairs if diag is None else [x + y for x, y in zip(diag, pairs)]
        gl_ref[own, :] = jnp.concatenate([diagonal_sums(d, 2 * tok)[:, :tok] for d in diag], axis=0)


def close_kernel(doc_ref, mg_ref, next_ref, x_ref, w_ref, out_ref, gs_ref, shifts, edge):
    tok, chunk = x_ref.shape
    wide = 2 * LANES

    @pl.when((pl.program_id(0) == 0) & (pl.program_id(1) == 0))
    def _():
        docs = near_docs(doc_ref, tok)
        own = docs[:, tok : 2 * tok]
        col = doc_column(own)
        shifts[0:tok, :] = shift_matrix(col, own, 1)
        shifts[tok:, :] = shift_matrix(col, own, 2)
        place = lax.broadcasted_iota(jnp.int32, (8, LANES), 0)
        new = [jnp.broadcast_to(docs[:, 2 * tok + d : 2 * tok + d + 1], (8, LANES)) for d in (0, 1)]
        final = col[tok - 8 :, :]
        edge[0] = jnp.where((place == 7) & (final == new[0]), 1.0, 0.0)
        edge[1] = jnp.where((place == 6) & (final == new[0]), 1.0, 0.0)
        edge[2] = jnp.where((place == 7) & (final == new[1]), 1.0, 0.0)

    edges = [jnp.concatenate([edge[i]] * 2, axis=1) for i in range(3)]
    for i in range(chunk // wide):
        at = slice(i * wide, (i + 1) * wide)
        g = mg_ref[0, :, at]
        moved = jnp.dot(shifts[...], g, preferred_element_type=F32)
        border = next_ref[0, :, at].astype(F32)
        one, two = moved[:tok], moved[tok:]
        one = jnp.concatenate([one[: tok - 8], one[tok - 8 :] + edges[0] * border[0:1]], axis=0)
        two = jnp.concatenate([two[: tok - 8], two[tok - 8 :] + edges[1] * border[0:1] + edges[2] * border[1:2]], axis=0)
        g = g.astype(F32)
        w = w_ref[:, at]
        out_ref[:, at] = (w[0:1] * g + w[1:2] * one + w[2:3] * two).astype(BF)
        x = x_ref[:, at].astype(F32)
        for tap, moved_grad in enumerate((g, one, two)):
            gs_ref[tap : tap + 1, at] = jnp.sum(moved_grad * x, axis=0, keepdims=True)


def reduce_kernel(depth, short_ref, long_ref, s_out, l_out, s1, l1, s2, l2, s3, l3, bs, bl, send, recv):
    dp, ctx = lax.axis_index("dp"), lax.axis_index("ctx")
    rows = lax.axis_size("dp")
    z, x, c = ctx // (ACROSS * CORES), (ctx // CORES) % ACROSS, ctx % CORES
    place = lambda zz, xx, cc: (zz * ACROSS + xx) * CORES + cc

    across = [(dp, place(z, (x + d) % ACROSS, c)) for d in range(1, ACROSS)]
    along = [(dp, place((z + d) % depth, x, c)) for d in range(1, depth)]
    final = []
    for d in range(1, rows * CORES):
        final.append(((dp + d // CORES) % rows, place(z, x, (c + d) % CORES)))
    peers = across + along + final
    barrier = pltpu.get_barrier_semaphore()
    for peer in peers:
        pl.semaphore_signal(barrier, inc=1, device_id=peer, device_id_type=MESH)
    pl.semaphore_wait(barrier, len(peers))

    def exchange(targets, sources, slot):
        copies = []
        for i, (peer, pairs) in enumerate(zip(targets, sources)):
            for j, (src, dst) in enumerate(pairs):
                at = 2 * (slot + i) + j
                copies.append(
                    pltpu.make_async_remote_copy(
                        src_ref=src, dst_ref=dst, send_sem=send.at[at], recv_sem=recv.at[at],
                        device_id=peer, device_id_type=MESH,
                    )
                )
        for copy in copies:
            copy.start()
        return copies

    def finish(copies):
        for copy in copies:
            copy.wait_recv()

    def total(first, arrived):
        for i in range(arrived.shape[0]):
            first = first + arrived[i]
        return first

    n1, n2, n3 = len(across), len(along), len(final)
    one = exchange(
        across,
        [
            [(short_ref.at[(x + d) % ACROSS], s1.at[d - 1]), (long_ref.at[(x + d) % ACROSS], l1.at[d - 1])]
            for d in range(1, ACROSS)
        ],
        0,
    )
    finish(one)
    bs[...] = total(short_ref[x], s1)
    bl[...] = total(long_ref[x], l1)
    two = exchange(
        along,
        [
            [(bs.at[(z + d) % depth], s2.at[d - 1]), (bl.at[(z + d) % depth], l2.at[d - 1])]
            for d in range(1, depth)
        ],
        n1,
    )
    finish(two)
    s3[n3] = total(bs[z], s2)
    l3[n3] = total(bl[z], l2)
    three = exchange(final, [[(s3.at[n3], s3.at[d]), (l3.at[n3], l3.at[d])] for d in range(n3)], n1 + n2)
    finish(three)
    s_out[...] = total(s3[n3], s3.at[pl.ds(0, n3)])
    l_out[...] = total(l3[n3], l3.at[pl.ds(0, n3)])
    for copy in one + two + three:
        copy.wait_send()


def mix_call(docs, x, border, w, cot, chunk):
    tok, width = cot.shape
    n = width // chunk
    third = [lambda i, p=p: (0, p * n + i) for p in range(3)]
    flat = lambda i: (0, i)
    shape = jax.ShapeDtypeStruct((tok, width), BF)
    return pl.pallas_call(
        mix_kernel,
        grid=(n,),
        out_shape=[shape] * 5,
        in_specs=[pl.BlockSpec(docs.shape, lambda i: (0, 0))]
        + [pl.BlockSpec((tok, chunk), m) for m in third]
        + [pl.BlockSpec((2, chunk), m) for m in third]
        + [pl.BlockSpec((3, chunk), m) for m in third]
        + [pl.BlockSpec((tok, chunk), flat)],
        out_specs=[pl.BlockSpec((tok, chunk), flat)] * 5,
        scratch_shapes=[pltpu.VMEM((2 * tok, tok), BF), pltpu.VMEM((3, 8, LANES), F32)],
        compiler_params=pltpu.CompilerParams(vmem_limit_bytes=VMEM),
        name="mix",
    )(docs, x, x, x, border, border, border, w, w, w, cot)


def long_call(docs, filt, q, k, v, cot, prod, gm, before, after, chunk):
    tok, width = cot.shape
    per = width // filt.shape[0]
    n = width // chunk
    flat = pl.BlockSpec((tok, chunk), lambda i: (0, i))
    return pl.pallas_call(
        functools.partial(long_kernel, LANES // per),
        grid=(n,),
        out_shape=[
            jax.ShapeDtypeStruct((tok, width), BF),
            jax.ShapeDtypeStruct((3, tok, width), BF),
            jax.ShapeDtypeStruct(filt.shape, F32),
        ],
        in_specs=[
            pl.BlockSpec(docs.shape, lambda i: (0, 0)),
            pl.BlockSpec((chunk // per, tok), lambda i: (i, 0)),
        ]
        + [flat] * 8,
        out_specs=[
            flat,
            pl.BlockSpec((3, tok, chunk), lambda i: (0, 0, i)),
            pl.BlockSpec((chunk // per, tok), lambda i: (i, 0)),
        ],
        scratch_shapes=[
            pltpu.VMEM((2 * tok, 2 * tok), BF),
            pltpu.VMEM((2 * tok, 2 * tok), F32),
            pltpu.VMEM((3 * tok, chunk), BF),
            pltpu.VMEM((3 * tok, chunk), BF),
            pltpu.VMEM((chunk // per, 4 * tok), F32),
        ],
        compiler_params=pltpu.CompilerParams(vmem_limit_bytes=VMEM),
        name="long",
    )(docs, filt, q, k, v, cot, prod, gm, before, after)


def close_call(docs, mg, ahead, x, w, chunk):
    tok, width = x.shape
    n = mg.shape[2] // chunk
    third = lambda p, i: (0, p * n + i)
    return pl.pallas_call(
        close_kernel,
        grid=(3, n),
        out_shape=[jax.ShapeDtypeStruct((tok, width), BF), jax.ShapeDtypeStruct((3, width), F32)],
        in_specs=[
            pl.BlockSpec(docs.shape, lambda p, i: (0, 0)),
            pl.BlockSpec((1, tok, chunk), lambda p, i: (p, 0, i)),
            pl.BlockSpec((1, 2, chunk), lambda p, i: (p, 0, i)),
            pl.BlockSpec((tok, chunk), third),
            pl.BlockSpec((3, chunk), third),
        ],
        out_specs=[pl.BlockSpec((tok, chunk), third), pl.BlockSpec((3, chunk), third)],
        scratch_shapes=[pltpu.VMEM((2 * tok, tok), BF), pltpu.VMEM((3, 8, LANES), F32)],
        compiler_params=pltpu.CompilerParams(vmem_limit_bytes=VMEM),
        name="close",
    )(docs, mg, ahead, x, w)


def reduce_call(gs, gl, dp, ctx):
    depth = ctx // (ACROSS * CORES)
    pair = gs.shape[1] // (ACROSS * depth)
    some = gl.shape[0] // (ACROSS * depth)
    taps = gl.shape[1]
    short = gs.reshape(3, depth, ACROSS, pair).transpose(2, 1, 0, 3)
    long = gl.reshape(depth, ACROSS, some, taps).transpose(1, 0, 2, 3)
    n3 = dp * CORES - 1
    total = (ACROSS - 1) + (depth - 1) + n3
    space = pl.BlockSpec(memory_space=pltpu.VMEM)
    vm = lambda *s: pltpu.VMEM(s, F32)
    return pl.pallas_call(
        functools.partial(reduce_kernel, depth),
        out_shape=[jax.ShapeDtypeStruct((3, pair), F32), jax.ShapeDtypeStruct((some, taps), F32)],
        in_specs=[space] * 2,
        out_specs=[space] * 2,
        scratch_shapes=[
            vm(ACROSS - 1, depth, 3, pair), vm(ACROSS - 1, depth, some, taps),
            vm(depth - 1, 3, pair), vm(depth - 1, some, taps),
            vm(n3 + 1, 3, pair), vm(n3 + 1, some, taps),
            vm(depth, 3, pair), vm(depth, some, taps),
            pltpu.SemaphoreType.DMA((2 * total,)),
            pltpu.SemaphoreType.DMA((2 * total,)),
        ],
        compiler_params=pltpu.CompilerParams(collective_id=0, has_side_effects=True, vmem_limit_bytes=VMEM),
        name="reduce",
    )(short, long)


def local(projected, doc_ids, short_filter, long_filter, cotangent):
    x, cot = projected[0], cotangent[0]
    tok, width = cot.shape
    groups, taps = long_filter.shape
    parts, rows = lax.axis_size("ctx"), lax.axis_size("dp")
    border = passed_along(x[tok - 2 :], "ctx", 1)
    q, k, v, prod, gm = mix_call(doc_ids, x, border, short_filter, cot, 512)
    before = passed_along(prod, "ctx", 1)
    after = passed_along(gm, "ctx", -1)
    out, mg, gl = long_call(doc_ids, long_filter, q, k, v, cot, prod, gm, before, after, 512)
    ahead = passed_along(mg[:, :2], "ctx", -1)
    gx, gs = close_call(doc_ids, mg, ahead, x, short_filter, 1024)
    gs, gl = reduce_call(gs, gl, rows, parts)
    core = lax.axis_index("ctx") % CORES
    gs = lax.dynamic_slice_in_dim(gs, core * (gs.shape[1] // CORES), gs.shape[1] // CORES, 1)
    gl = lax.dynamic_slice_in_dim(gl, core * (gl.shape[0] // CORES), gl.shape[0] // CORES, 0)
    norm = rows * doc_ids.shape[1]
    return out[None], gx[None], gs / math.sqrt(norm), gl / math.sqrt(norm * (width // groups))


def solution(mesh):
    return jax.shard_map(
        local,
        mesh=mesh,
        in_specs=(P("dp", "ctx", None), P("dp", None), P(), P(), P("dp", "ctx", None)),
        out_specs=(P("dp", "ctx", None), P("dp", "ctx", None), P(None, "ctx"), P("ctx", None)),
        check_vma=False,
    )
```

```python
import functools
import math

import jax
import jax.numpy as jnp
from jax import lax
from jax.experimental import pallas as pl
from jax.experimental.pallas import tpu as pltpu
from jax.sharding import PartitionSpec as P

BF = jnp.bfloat16
F32 = jnp.float32
MESH = pl.DeviceIdType.MESH
ROWS = 16
LANES = 128
CORES = 2
ACROSS = 4
VMEM = 56 << 20


def near_docs(doc_ref, tok):
    me = lax.axis_index("ctx")
    last = lax.axis_size("ctx") - 1
    at = lambda i: doc_ref[:, pl.ds(pl.multiple_of(i * tok, tok), tok)]
    before = jnp.where(me > 0, at(jnp.maximum(me - 1, 0)), -1)
    after = jnp.where(me < last, at(jnp.minimum(me + 1, last)), -2)
    return jnp.concatenate([before, at(me), after], axis=1).astype(F32)


def doc_column(row):
    return jnp.broadcast_to(row, (row.shape[1], row.shape[1])).T


def shift_matrix(col, row, steps):
    size = col.shape[0]
    place = lax.broadcasted_iota(jnp.int32, (size, size), 1) - lax.broadcasted_iota(jnp.int32, (size, size), 0)
    return jnp.where((place == steps) & (col == row), 1.0, 0.0).astype(BF)


def ring(steps):
    size = lax.axis_size("ctx")
    return lax.axis_index("dp"), (lax.axis_index("ctx") + size + steps) % size


def greet(peers):
    barrier = pltpu.get_barrier_semaphore()
    for peer in peers:
        pl.semaphore_signal(barrier, inc=1, device_id=peer, device_id_type=MESH)
    pl.semaphore_wait(barrier, len(peers))


def sent(src, dst, send, recv, peer):
    return pltpu.make_async_remote_copy(
        src_ref=src, dst_ref=dst, send_sem=send, recv_sem=recv, device_id=peer, device_id_type=MESH
    )


def mix_kernel(chunk, doc_ref, w_ref, x_hbm, cot_hbm, q_out, k_out, v_out, prod_out, gm_out, before_out, after_out,
               xs, cs, tail, mine, border, qs, ks, vs, ps, gs, shifts, edge,
               tail_sem, in_sem, out_sem, edge_sem, send, recv):
    tok, width = cs.shape
    wide = 2 * LANES
    count = width // chunk
    right, left = ring(1), ring(-1)

    def at(i, size=chunk, offset=0):
        return pl.ds(pl.multiple_of(offset + i * size, LANES), size)

    def loads(i):
        for p in range(3):
            here = at(i, offset=p * width)
            yield pltpu.make_async_copy(x_hbm.at[:, here], xs.at[:, here], in_sem.at[p, i])
        yield pltpu.make_async_copy(cot_hbm.at[:, at(i)], cs.at[:, at(i)], in_sem.at[3, i])

    def saves(i):
        pairs = ((qs, q_out), (ks, k_out), (vs, v_out), (ps, prod_out), (gs, gm_out))
        for p, (src, dst) in enumerate(pairs):
            yield pltpu.make_async_copy(src.at[:, at(i)], dst.at[:, at(i)], out_sem.at[p, i])

    def sends(i):
        yield sent(ps.at[:, at(i)], before_out.at[:, at(i)], send.at[0, i], recv.at[0, i], right)
        yield sent(gs.at[:, at(i)], after_out.at[:, at(i)], send.at[1, i], recv.at[1, i], left)

    first = pltpu.make_async_copy(x_hbm.at[tok - 16 :, :], tail, tail_sem)
    first.start()
    for i in range(count):
        for copy in loads(i):
            copy.start()
    docs = near_docs(doc_ref, tok)
    own = docs[:, tok : 2 * tok]
    col = doc_column(own)
    shifts[0:tok, :] = shift_matrix(col, own, -1)
    shifts[tok:, :] = shift_matrix(col, own, -2)
    place = lax.broadcasted_iota(jnp.int32, (8, LANES), 0)
    old = [jnp.broadcast_to(docs[:, tok - d : tok - d + 1], (8, LANES)) for d in (1, 2)]
    head = col[:8, :]
    edge[0] = jnp.where((place == 0) & (head == old[0]), 1.0, 0.0)
    edge[1] = jnp.where((place == 0) & (head == old[1]), 1.0, 0.0)
    edge[2] = jnp.where((place == 1) & (head == old[0]), 1.0, 0.0)
    first.wait()
    mine[...] = tail[14:16, :]
    greet([right, left])
    edge_copy = sent(mine, border, edge_sem.at[0], edge_sem.at[1], right)
    edge_copy.start()
    edge_copy.wait()

    def mixed(i, j, part):
        here = pl.ds(pl.multiple_of(part * width + i * chunk + j * wide, LANES), wide)
        edges = [jnp.concatenate([edge[n]] * 2, axis=1) for n in range(3)]
        x = xs[:, here]
        moved = jnp.dot(shifts[...], x, preferred_element_type=F32)
        side = border[:, here].astype(F32)
        w = w_ref[:, here]
        total = w[0:1] * x.astype(F32) + w[1:2] * moved[:tok] + w[2:3] * moved[tok:]
        fix = w[1:2] * (edges[0] * side[1:2]) + w[2:3] * (edges[1] * side[0:1] + edges[2] * side[1:2])
        return jnp.concatenate([total[:8] + fix, total[8:]], axis=0).astype(BF)

    def step(i, carry):
        for copy in loads(i):
            copy.wait()
        for j in range(chunk // wide):
            here = pl.ds(pl.multiple_of(i * chunk + j * wide, LANES), wide)
            q, k, v = mixed(i, j, 0), mixed(i, j, 1), mixed(i, j, 2)
            qs[:, here], ks[:, here], vs[:, here] = q, k, v
            gs[:, here] = (cs[:, here].astype(F32) * q.astype(F32)).astype(BF)
            ps[:, here] = (k.astype(F32) * v.astype(F32)).astype(BF)
        for copy in sends(i):
            copy.start()
        for copy in saves(i):
            copy.start()
        return carry

    lax.fori_loop(0, count, step, 0)

    def drain(i, carry):
        for copy in saves(i):
            copy.wait()
        for copy in sends(i):
            copy.wait()
        return carry

    lax.fori_loop(0, count, drain, 0)


def banded(filt, rows):
    parts = []
    for g in range(filt.shape[0]):
        wide = jnp.broadcast_to(filt[g : g + 1, :], (rows, filt.shape[1]))
        parts.append(pltpu.roll(wide, 0, 1, stride=1, stride_axis=0).astype(BF))
    return parts


def diagonal_sums(part, width):
    half = part.shape[0] // 2
    while half >= 8:
        part = part[:half] + pltpu.roll(part[half:], width - half, 1)
        half //= 2
    while half >= 1:
        part = part + pltpu.roll(pltpu.roll(part, 8 - half, 0), width - half, 1)
        half //= 2
    return part[0:1]


def long_kernel(groups, doc_ref, filt_ref, q_ref, k_ref, v_ref, cot_ref, prod_ref, gm_ref,
                before_ref, after_ref, out_ref, mg_ref, gl_ref, keeps, keeps32, pwin, gwin, wide):
    rows = ROWS
    tok, width = q_ref.shape
    steps = tok // rows
    lane_group = lax.broadcasted_iota(jnp.int32, (rows, LANES), 1) // (LANES // groups)

    @pl.when(pl.program_id(0) == 0)
    def _():
        docs = near_docs(doc_ref, tok)
        col = doc_column(docs[:, tok : 2 * tok])
        col = jnp.concatenate([col, col], axis=1)
        row = jnp.concatenate([jnp.broadcast_to(docs, (8, 3 * tok)), jnp.full((8, tok), -3.0, F32)], axis=1)
        for a in range(steps):
            mine = col[a * rows : (a + 1) * rows]
            for b, start in ((a, a * rows), (steps + a, tok + a * rows)):
                window = pltpu.roll(row, (4 * tok - start) % (4 * tok), 1)[0:1, : 2 * tok]
                keep = jnp.where(mine == window, 1.0, 0.0)
                keeps32[b * rows : (b + 1) * rows, :] = keep
                keeps[b * rows : (b + 1) * rows, :] = keep.astype(BF)
        pwin[2 * tok :, :] = jnp.zeros((tok, width), BF)
        gwin[2 * tok :, :] = jnp.zeros((tok, width), BF)

    pwin[0:tok, :] = before_ref[...]
    pwin[tok : 2 * tok, :] = prod_ref[...]
    gwin[0:tok, :] = gm_ref[...]
    gwin[tok : 2 * tok, :] = after_ref[...]
    filt = filt_ref[...]
    total = filt.shape[0]
    turn = lax.broadcasted_iota(jnp.int32, (tok, tok), 0) + lax.broadcasted_iota(jnp.int32, (tok, tok), 1)
    turned = jnp.dot(filt, jnp.where(turn == tok, 1.0, 0.0).astype(BF), preferred_element_type=F32)
    filt = filt.astype(F32)
    lane = lax.broadcasted_iota(jnp.int32, (total, tok), 1)
    wide[:, 0:tok] = turned
    wide[:, tok : 2 * tok] = jnp.where(lane == 0, filt, 0.0)
    wide[:, 2 * tok : 3 * tok] = filt
    wide[:, 3 * tok :] = jnp.zeros((total, tok), F32)

    def pick(value):
        chosen = value[:rows]
        for g in range(1, groups):
            chosen = jnp.where(lane_group == g, value[g * rows : (g + 1) * rows], chosen)
        return chosen

    for i in range(width // LANES):
        at = slice(i * LANES, (i + 1) * LANES)
        own = slice(i * groups, (i + 1) * groups)
        ahead = banded(wide[own, : 2 * tok], rows)
        back = banded(wide[own, 2 * tok :], rows)
        diag = None
        for a in range(steps):
            here = slice(a * rows, (a + 1) * rows)
            there = slice((steps + a) * rows, (steps + a + 1) * rows)
            span = slice(a * rows, a * rows + 2 * tok)
            keep = keeps[here, :]
            mix = jnp.dot(jnp.concatenate([b * keep for b in ahead], axis=0), pwin[span, at], preferred_element_type=F32)
            mix = pick(mix).astype(BF).astype(F32)
            out_ref[here, at] = (q_ref[here, at].astype(F32) * mix).astype(BF)
            mg_ref[0, here, at] = (cot_ref[here, at].astype(F32) * mix).astype(BF)
            keep = keeps[there, :]
            grad = jnp.dot(jnp.concatenate([b * keep for b in back], axis=0), gwin[span, at], preferred_element_type=F32)
            grad = pick(grad).astype(BF).astype(F32)
            mg_ref[1, here, at] = (grad * v_ref[here, at].astype(F32)).astype(BF)
            mg_ref[2, here, at] = (grad * k_ref[here, at].astype(F32)).astype(BF)
            mine = prod_ref[here, at]
            zero = jnp.zeros_like(mine)
            spread = jnp.concatenate([jnp.where(lane_group == g, mine, zero) for g in range(groups)], axis=0)
            pairs = lax.dot_general(spread, gwin[span, at], (((1,), (1,)), ((), ())), preferred_element_type=F32)
            keep = keeps32[there, :]
            pairs = [pairs[g * rows : (g + 1) * rows] * keep for g in range(groups)]
            diag = pairs if diag is None else [x + y for x, y in zip(diag, pairs)]
        gl_ref[own, :] = jnp.concatenate([diagonal_sums(d, 2 * tok)[:, :tok] for d in diag], axis=0)


def close_kernel(depth, piece, doc_ref, w_ref, long_ref, mg_hbm, x_hbm, gx_out, s_out, l_out,
                 xs, gs, ys, heads, mine, ahead, shifts, edge, sums,
                 s1, l1, s2, l2, s3, l3, bs, bl, head_sem, g_sem, x_sem, y_sem, row_sem, send, recv):
    tok, full = xs.shape
    width = full // 3
    chunk = full // depth
    pair = chunk // ACROSS
    dp, ctx = lax.axis_index("dp"), lax.axis_index("ctx")
    rows = lax.axis_size("dp")
    z, x, c = ctx // (ACROSS * CORES), (ctx // CORES) % ACROSS, ctx % CORES
    place = lambda zz, xx, cc: (zz * ACROSS + xx) * CORES + cc
    across = [(dp, place(z, (x + d) % ACROSS, c)) for d in range(1, ACROSS)]
    along = [(dp, place((z + d) % depth, x, c)) for d in range(1, depth)]
    final = [((dp + d // CORES) % rows, place(z, x, (c + d) % CORES)) for d in range(1, rows * CORES)]
    n1, n2, n3 = len(across), len(along), len(final)
    right, left = ring(1), ring(-1)

    def flat(i, size):
        return pl.ds(pl.multiple_of(i * size, LANES), size)

    per = width // piece

    def g_load(n):
        src = mg_hbm.at[n // per, :, flat(n % per, piece)]
        return pltpu.make_async_copy(src, gs.at[:, flat(n, piece)], g_sem.at[n])

    def x_load(i):
        return pltpu.make_async_copy(x_hbm.at[:, flat(i, chunk)], xs.at[:, flat(i, chunk)], x_sem.at[i])

    def y_save(i):
        return pltpu.make_async_copy(ys.at[:, flat(i, chunk)], gx_out.at[:, flat(i, chunk)], y_sem.at[i])

    def first_exchange(src, dst, k):
        return [sent(src.at[(x + d) % ACROSS], dst.at[d - 1], send.at[k, d - 1], recv.at[k, d - 1], across[d - 1])
                for d in range(1, ACROSS)]

    def second_exchange(src, dst, k):
        return [sent(src.at[(z + d) % depth], dst.at[d - 1], send.at[k, n1 + d - 1], recv.at[k, n1 + d - 1], along[d - 1])
                for d in range(1, depth)]

    def third_exchange(buf, k):
        return [sent(buf.at[n3], buf.at[d], send.at[k, n1 + n2 + d], recv.at[k, n1 + n2 + d], final[d])
                for d in range(n3)]

    def begin(copies):
        for copy in copies:
            copy.start()

    def arrive(copies):
        for copy in copies:
            copy.wait_recv()

    def total(start, arrived, n):
        for i in range(n):
            start = start + arrived[i]
        return start

    head = pltpu.make_async_copy(mg_hbm.at[:, 0:16, :], heads, head_sem)
    head.start()
    for i in range(depth):
        x_load(i).start()
        for n in range(i * chunk // piece, (i + 1) * chunk // piece):
            g_load(n).start()
    docs = near_docs(doc_ref, tok)
    own = docs[:, tok : 2 * tok]
    col = doc_column(own)
    shifts[0:tok, :] = shift_matrix(col, own, 1)
    shifts[tok:, :] = shift_matrix(col, own, 2)
    row = lax.broadcasted_iota(jnp.int32, (8, LANES), 0)
    new = [jnp.broadcast_to(docs[:, 2 * tok + d : 2 * tok + d + 1], (8, LANES)) for d in (0, 1)]
    end = col[tok - 8 :, :]
    edge[0] = jnp.where((row == 7) & (end == new[0]), 1.0, 0.0)
    edge[1] = jnp.where((row == 6) & (end == new[0]), 1.0, 0.0)
    edge[2] = jnp.where((row == 7) & (end == new[1]), 1.0, 0.0)
    head.wait()
    for p in range(3):
        mine[:, p * width : (p + 1) * width] = heads[p, 0:2, :]
    greet([right, left] + across + along + final)
    row_copy = sent(mine, ahead, row_sem.at[0], row_sem.at[1], left)
    row_copy.start()
    long_one = first_exchange(long_ref, l1, 1)
    begin(long_one)
    row_copy.wait()

    def step(i, carry):
        x_load(i).wait()
        for n in range(chunk // piece):
            g_load(i * (chunk // piece) + n).wait()
        edges = [jnp.concatenate([edge[n]] * (pair // LANES), axis=1) for n in range(3)]
        for j in range(ACROSS):
            here = pl.ds(pl.multiple_of(i * chunk + j * pair, LANES), pair)
            g = gs[:, here]
            moved = jnp.dot(shifts[...], g, preferred_element_type=F32)
            side = ahead[:, here].astype(F32)
            one, two = moved[:tok], moved[tok:]
            one = jnp.concatenate([one[: tok - 8], one[tok - 8 :] + edges[0] * side[0:1]], axis=0)
            two = jnp.concatenate(
                [two[: tok - 8], two[tok - 8 :] + edges[1] * side[0:1] + edges[2] * side[1:2]], axis=0
            )
            g = g.astype(F32)
            w = w_ref[:, here]
            ys[:, here] = (w[0:1] * g + w[1:2] * one + w[2:3] * two).astype(BF)
            source = xs[:, here].astype(F32)
            sums[j, i] = jnp.concatenate(
                [jnp.sum(moved_grad * source, axis=0, keepdims=True) for moved_grad in (g, one, two)], axis=0
            )
        y_save(i).start()
        return carry

    half = depth // 2
    lax.fori_loop(0, half, step, 0)
    arrive(long_one)
    bl[...] = total(long_ref[x], l1, n1)
    long_two = second_exchange(bl, l2, 1)
    begin(long_two)
    lax.fori_loop(half, depth, step, 0)
    short_one = first_exchange(sums, s1, 0)
    begin(short_one)
    arrive(long_two)
    l3[n3] = total(bl[z], l2, n2)
    long_three = third_exchange(l3, 1)
    begin(long_three)
    arrive(short_one)
    bs[...] = total(sums[x], s1, n1)
    short_two = second_exchange(bs, s2, 0)
    begin(short_two)
    arrive(long_three)
    l_out[...] = total(l3[n3], l3, n3)
    arrive(short_two)
    s3[n3] = total(bs[z], s2, n2)
    short_three = third_exchange(s3, 0)
    begin(short_three)
    for i in range(depth):
        y_save(i).wait()
    arrive(short_three)
    s_out[...] = total(s3[n3], s3, n3)
    for copy in long_one + long_two + long_three + short_one + short_two + short_three:
        copy.wait_send()


def mix_call(docs, x, w, cot, chunk):
    tok, width = cot.shape
    n = width // chunk
    shape = jax.ShapeDtypeStruct((tok, width), BF)
    space, far = pl.BlockSpec(memory_space=pltpu.VMEM), pl.BlockSpec(memory_space=pl.ANY)
    dma = pltpu.SemaphoreType.DMA
    return pl.pallas_call(
        functools.partial(mix_kernel, chunk),
        out_shape=[shape] * 7,
        in_specs=[space, space, far, far],
        out_specs=[far] * 7,
        scratch_shapes=[
            pltpu.VMEM((tok, 3 * width), BF), pltpu.VMEM((tok, width), BF), pltpu.VMEM((16, 3 * width), BF),
            pltpu.VMEM((2, 3 * width), BF), pltpu.VMEM((2, 3 * width), BF),
        ]
        + [pltpu.VMEM((tok, width), BF)] * 5
        + [
            pltpu.VMEM((2 * tok, tok), BF), pltpu.VMEM((3, 8, LANES), F32),
            dma, dma((4, n)), dma((5, n)), dma((2,)), dma((2, n)), dma((2, n)),
        ],
        compiler_params=pltpu.CompilerParams(collective_id=0, has_side_effects=True, vmem_limit_bytes=VMEM),
        name="mix",
    )(docs, w, x, cot)


def long_call(docs, filt, q, k, v, cot, prod, gm, before, after, chunk):
    tok, width = cot.shape
    per = width // filt.shape[0]
    n = width // chunk
    flat = pl.BlockSpec((tok, chunk), lambda i: (0, i))
    return pl.pallas_call(
        functools.partial(long_kernel, LANES // per),
        grid=(n,),
        out_shape=[
            jax.ShapeDtypeStruct((tok, width), BF),
            jax.ShapeDtypeStruct((3, tok, width), BF),
            jax.ShapeDtypeStruct(filt.shape, F32),
        ],
        in_specs=[
            pl.BlockSpec(docs.shape, lambda i: (0, 0)),
            pl.BlockSpec((chunk // per, tok), lambda i: (i, 0)),
        ]
        + [flat] * 8,
        out_specs=[
            flat,
            pl.BlockSpec((3, tok, chunk), lambda i: (0, 0, i)),
            pl.BlockSpec((chunk // per, tok), lambda i: (i, 0)),
        ],
        scratch_shapes=[
            pltpu.VMEM((2 * tok, 2 * tok), BF),
            pltpu.VMEM((2 * tok, 2 * tok), F32),
            pltpu.VMEM((3 * tok, chunk), BF),
            pltpu.VMEM((3 * tok, chunk), BF),
            pltpu.VMEM((chunk // per, 4 * tok), F32),
        ],
        compiler_params=pltpu.CompilerParams(vmem_limit_bytes=VMEM),
        name="long",
    )(docs, filt, q, k, v, cot, prod, gm, before, after)


def close_call(docs, mg, x, w, gl, dp, ctx):
    tok, full = x.shape
    depth = ctx // (ACROSS * CORES)
    pair = full // (ACROSS * depth)
    some = gl.shape[0] // (ACROSS * depth)
    taps = gl.shape[1]
    long = gl.reshape(depth, ACROSS, some, taps).transpose(1, 0, 2, 3)
    n3 = dp * CORES - 1
    n = (ACROSS - 1) + (depth - 1) + n3
    piece = 4 * LANES
    space, far = pl.BlockSpec(memory_space=pltpu.VMEM), pl.BlockSpec(memory_space=pl.ANY)
    dma = pltpu.SemaphoreType.DMA
    vm = lambda *s: pltpu.VMEM(s, F32)
    return pl.pallas_call(
        functools.partial(close_kernel, depth, piece),
        out_shape=[
            jax.ShapeDtypeStruct((tok, full), BF),
            jax.ShapeDtypeStruct((3, pair), F32),
            jax.ShapeDtypeStruct((some, taps), F32),
        ],
        in_specs=[space] * 3 + [far] * 2,
        out_specs=[far, space, space],
        scratch_shapes=[
            pltpu.VMEM((tok, full), BF), pltpu.VMEM((tok, full), BF), pltpu.VMEM((tok, full), BF),
            pltpu.VMEM((3, 16, full // 3), BF), pltpu.VMEM((2, full), BF), pltpu.VMEM((2, full), BF),
            pltpu.VMEM((2 * tok, tok), BF), vm(3, 8, LANES), vm(ACROSS, depth, 3, pair),
            vm(ACROSS - 1, depth, 3, pair), vm(ACROSS - 1, depth, some, taps),
            vm(depth - 1, 3, pair), vm(depth - 1, some, taps),
            vm(n3 + 1, 3, pair), vm(n3 + 1, some, taps),
            vm(depth, 3, pair), vm(depth, some, taps),
            dma, dma((full // piece,)), dma((depth,)), dma((depth,)), dma((2,)), dma((2, n)), dma((2, n)),
        ],
        compiler_params=pltpu.CompilerParams(collective_id=1, has_side_effects=True, vmem_limit_bytes=VMEM),
        name="close",
    )(docs, w, long, mg, x)


def local(projected, doc_ids, short_filter, long_filter, cotangent):
    x, cot = projected[0], cotangent[0]
    tok, width = cot.shape
    groups, taps = long_filter.shape
    parts, rows = lax.axis_size("ctx"), lax.axis_size("dp")
    q, k, v, prod, gm, before, after = mix_call(doc_ids, x, short_filter, cot, 512)
    out, mg, gl = long_call(doc_ids, long_filter, q, k, v, cot, prod, gm, before, after, 512)
    gx, gs, gl = close_call(doc_ids, mg, x, short_filter, gl, rows, parts)
    core = lax.axis_index("ctx") % CORES
    gs = lax.dynamic_slice_in_dim(gs, core * (gs.shape[1] // CORES), gs.shape[1] // CORES, 1)
    gl = lax.dynamic_slice_in_dim(gl, core * (gl.shape[0] // CORES), gl.shape[0] // CORES, 0)
    norm = rows * doc_ids.shape[1]
    return out[None], gx[None], gs / math.sqrt(norm), gl / math.sqrt(norm * (width // groups))


def solution(mesh):
    return jax.shard_map(
        local,
        mesh=mesh,
        in_specs=(P("dp", "ctx", None), P("dp", None), P(), P(), P("dp", "ctx", None)),
        out_specs=(P("dp", "ctx", None), P("dp", "ctx", None), P(None, "ctx"), P("ctx", None)),
        check_vma=False,
    )
```

```python
import functools
import math

import jax
import jax.numpy as jnp
from jax import lax
from jax.experimental import pallas as pl
from jax.experimental.pallas import tpu as pltpu
from jax.sharding import PartitionSpec as P

BF = jnp.bfloat16
F32 = jnp.float32
MESH = pl.DeviceIdType.MESH
ROWS = 16
LANES = 128
CORES = 2
ACROSS = 4
VMEM = 56 << 20


def near_docs(doc_ref, tok):
    me = lax.axis_index("ctx")
    last = lax.axis_size("ctx") - 1
    at = lambda i: doc_ref[:, pl.ds(pl.multiple_of(i * tok, tok), tok)]
    before = jnp.where(me > 0, at(jnp.maximum(me - 1, 0)), -1)
    after = jnp.where(me < last, at(jnp.minimum(me + 1, last)), -2)
    return jnp.concatenate([before, at(me), after], axis=1).astype(F32)


def doc_column(row):
    return jnp.broadcast_to(row, (row.shape[1], row.shape[1])).T


def shift_matrix(col, row, steps):
    size = col.shape[0]
    place = lax.broadcasted_iota(jnp.int32, (size, size), 1) - lax.broadcasted_iota(jnp.int32, (size, size), 0)
    return jnp.where((place == steps) & (col == row), 1.0, 0.0).astype(BF)


def ring(steps):
    size = lax.axis_size("ctx")
    return lax.axis_index("dp"), (lax.axis_index("ctx") + size + steps) % size


def greet(peers):
    barrier = pltpu.get_barrier_semaphore()
    for peer in peers:
        pl.semaphore_signal(barrier, inc=1, device_id=peer, device_id_type=MESH)
    pl.semaphore_wait(barrier, len(peers))


def sent(src, dst, send, recv, peer):
    return pltpu.make_async_remote_copy(
        src_ref=src, dst_ref=dst, send_sem=send, recv_sem=recv, device_id=peer, device_id_type=MESH
    )


def banded(filt, rows):
    parts = []
    for g in range(filt.shape[0]):
        wide = jnp.broadcast_to(filt[g : g + 1, :], (rows, filt.shape[1]))
        parts.append(pltpu.roll(wide, 0, 1, stride=1, stride_axis=0).astype(BF))
    return parts


def diagonal_sums(part, width):
    half = part.shape[0] // 2
    while half >= 8:
        part = part[:half] + pltpu.roll(part[half:], width - half, 1)
        half //= 2
    while half >= 1:
        part = part + pltpu.roll(pltpu.roll(part, 8 - half, 0), width - half, 1)
        half //= 2
    return part[0:1]


def whole_kernel(groups, chunk, depth, scales, doc_ref, w_ref, filt_ref, x_hbm, cot_hbm, out_hbm, gx_hbm, s_out, l_out,
                 xs, cs, qs, ks, vs, pwin, gwin, mg, ys, outs, tail, mine, border, heads, ahead,
                 back_shift, fore_shift, back_edge, fore_edge, keeps, keeps32, wide_filt, ssum, lsum,
                 s1, l1, s2, l2, s3, l3, bs, bl,
                 tail_sem, in_sem, out_sem, y_sem, edge_sem, blk_send, blk_recv, row_send, row_recv, send, recv):
    rows = ROWS
    tok, width = cs.shape
    full = 3 * width
    steps = tok // rows
    count = width // chunk
    blocks = chunk // LANES
    wide = 2 * LANES
    dp, ctx = lax.axis_index("dp"), lax.axis_index("ctx")
    z, x, c = ctx // (ACROSS * CORES), (ctx // CORES) % ACROSS, ctx % CORES
    place = lambda zz, xx, cc: (zz * ACROSS + xx) * CORES + cc
    dps = lax.axis_size("dp")
    across = [(dp, place(z, (x + d) % ACROSS, c)) for d in range(1, ACROSS)]
    along = [(dp, place((z + d) % depth, x, c)) for d in range(1, depth)]
    final = [((dp + d // CORES) % dps, place(z, x, (c + d) % CORES)) for d in range(1, dps * CORES)]
    n1, n2, n3 = len(across), len(along), len(final)
    right, left = ring(1), ring(-1)

    def at(i, size=chunk, offset=0):
        return pl.ds(pl.multiple_of(offset + i * size, LANES), size)

    def loads(i):
        for p in range(3):
            here = at(i, offset=p * width)
            yield pltpu.make_async_copy(x_hbm.at[:, here], xs.at[:, here], in_sem.at[p, i])
        yield pltpu.make_async_copy(cot_hbm.at[:, at(i)], cs.at[:, at(i)], in_sem.at[3, i])

    def block_sends(i):
        own = pl.ds(tok, tok), pl.ds(0, tok)
        yield sent(pwin.at[own[0], at(i)], pwin.at[own[1], at(i)], blk_send.at[0, i], blk_recv.at[0, i], right)
        yield sent(gwin.at[own[1], at(i)], gwin.at[own[0], at(i)], blk_send.at[1, i], blk_recv.at[1, i], left)

    def row_sends(i):
        for p in range(3):
            here = at(i, offset=p * width)
            yield sent(heads.at[:, here], ahead.at[:, here], row_send.at[p, i], row_recv.at[p, i], left)

    def out_save(i):
        return pltpu.make_async_copy(outs.at[:, at(i)], out_hbm.at[:, at(i)], out_sem.at[i])

    slab = full // depth

    def y_save(i):
        return pltpu.make_async_copy(ys.at[:, at(i, slab)], gx_hbm.at[:, at(i, slab)], y_sem.at[i])

    def first_exchange(src, dst, k):
        return [sent(src.at[(x + d) % ACROSS], dst.at[d - 1], send.at[k, d - 1], recv.at[k, d - 1], across[d - 1])
                for d in range(1, ACROSS)]

    def second_exchange(src, dst, k):
        return [sent(src.at[(z + d) % depth], dst.at[d - 1], send.at[k, n1 + d - 1], recv.at[k, n1 + d - 1], along[d - 1])
                for d in range(1, depth)]

    def third_exchange(buf, k):
        return [sent(buf.at[n3], buf.at[d], send.at[k, n1 + n2 + d], recv.at[k, n1 + n2 + d], final[d])
                for d in range(n3)]

    def begin(copies):
        for copy in copies:
            copy.start()

    def arrive(copies):
        for copy in copies:
            copy.wait_recv()

    def total(start, arrived, n):
        for i in range(n):
            start = start + arrived[i]
        return start

    first = pltpu.make_async_copy(x_hbm.at[tok - 16 :, :], tail, tail_sem)
    first.start()
    for i in range(count):
        begin(loads(i))
    peers = [right, left] + across + along + final
    barrier = pltpu.get_barrier_semaphore()
    for peer in peers:
        pl.semaphore_signal(barrier, inc=1, device_id=peer, device_id_type=MESH)
    first.wait()
    mine[...] = tail[14:16, :]
    pl.semaphore_wait(barrier, len(peers))
    edge_copy = sent(mine, border, edge_sem.at[0], edge_sem.at[1], right)
    edge_copy.start()

    docs = near_docs(doc_ref, tok)
    own = docs[:, tok : 2 * tok]
    col = doc_column(own)
    for shifts, sign in ((back_shift, -1), (fore_shift, 1)):
        shifts[0:tok, :] = shift_matrix(col, own, sign)
        shifts[tok:, :] = shift_matrix(col, own, 2 * sign)
    row = lax.broadcasted_iota(jnp.int32, (8, LANES), 0)
    spread_doc = lambda d: jnp.broadcast_to(docs[:, d : d + 1], (8, LANES))
    top, end = col[:8, :], col[tok - 8 :, :]
    old, new = [spread_doc(tok - 1), spread_doc(tok - 2)], [spread_doc(2 * tok), spread_doc(2 * tok + 1)]
    back_edge[0] = jnp.where((row == 0) & (top == old[0]), 1.0, 0.0)
    back_edge[1] = jnp.where((row == 0) & (top == old[1]), 1.0, 0.0)
    back_edge[2] = jnp.where((row == 1) & (top == old[0]), 1.0, 0.0)
    fore_edge[0] = jnp.where((row == 7) & (end == new[0]), 1.0, 0.0)
    fore_edge[1] = jnp.where((row == 6) & (end == new[0]), 1.0, 0.0)
    fore_edge[2] = jnp.where((row == 7) & (end == new[1]), 1.0, 0.0)
    edge_copy.wait()

    def mixed(i, j, part):
        here = pl.ds(pl.multiple_of(part * width + i * chunk + j * wide, LANES), wide)
        edges = [jnp.concatenate([back_edge[n]] * 2, axis=1) for n in range(3)]
        value = xs[:, here]
        moved = jnp.dot(back_shift[...], value, preferred_element_type=F32)
        side = border[:, here].astype(F32)
        w = w_ref[:, here]
        mix = w[0:1] * value.astype(F32) + w[1:2] * moved[:tok] + w[2:3] * moved[tok:]
        fix = w[1:2] * (edges[0] * side[1:2]) + w[2:3] * (edges[1] * side[0:1] + edges[2] * side[1:2])
        return jnp.concatenate([mix[:8] + fix, mix[8:]], axis=0).astype(BF)

    def mix_step(i, carry):
        for copy in loads(i):
            copy.wait()
        for j in range(chunk // wide):
            here = pl.ds(pl.multiple_of(i * chunk + j * wide, LANES), wide)
            q, k, v = mixed(i, j, 0), mixed(i, j, 1), mixed(i, j, 2)
            qs[:, here], ks[:, here], vs[:, here] = q, k, v
            gwin[0:tok, here] = (cs[:, here].astype(F32) * q.astype(F32)).astype(BF)
            pwin[tok : 2 * tok, here] = (k.astype(F32) * v.astype(F32)).astype(BF)
        begin(block_sends(i))
        return carry

    lax.fori_loop(0, count, mix_step, 0)

    both = jnp.concatenate([col, col], axis=1)
    long_row = jnp.concatenate([jnp.broadcast_to(docs, (8, 3 * tok)), jnp.full((8, tok), -3.0, F32)], axis=1)
    for a in range(steps):
        block_docs = both[a * rows : (a + 1) * rows]
        for b, start in ((a, a * rows), (steps + a, tok + a * rows)):
            window = pltpu.roll(long_row, (4 * tok - start) % (4 * tok), 1)[0:1, : 2 * tok]
            keep = jnp.where(block_docs == window, 1.0, 0.0)
            keeps32[b * rows : (b + 1) * rows, :] = keep
            keeps[b * rows : (b + 1) * rows, :] = keep.astype(BF)
    pwin[2 * tok :, :] = jnp.zeros((tok, width), BF)
    gwin[2 * tok :, :] = jnp.zeros((tok, width), BF)
    filt = filt_ref[...]
    turn = lax.broadcasted_iota(jnp.int32, (tok, tok), 0) + lax.broadcasted_iota(jnp.int32, (tok, tok), 1)
    wide_filt[:, 0:tok] = jnp.dot(filt, jnp.where(turn == tok, 1.0, 0.0).astype(BF), preferred_element_type=F32)
    filt = filt.astype(F32)
    lane = lax.broadcasted_iota(jnp.int32, filt.shape, 1)
    wide_filt[:, tok : 2 * tok] = jnp.where(lane == 0, filt, 0.0)
    wide_filt[:, 2 * tok : 3 * tok] = filt
    wide_filt[:, 3 * tok :] = jnp.zeros(filt.shape, F32)

    lane_group = lax.broadcasted_iota(jnp.int32, (rows, LANES), 1) // (LANES // groups)

    def pick(value):
        chosen = value[:rows]
        for g in range(1, groups):
            chosen = jnp.where(lane_group == g, value[g * rows : (g + 1) * rows], chosen)
        return chosen

    per_z = count * blocks // depth
    per_x = per_z // ACROSS

    def long_step(i, carry):
        arrive(block_sends(i))
        for j in range(blocks):
            part = [pl.ds(pl.multiple_of(p * width + i * chunk + j * LANES, LANES), LANES) for p in range(3)]
            here = part[0]
            b = i * blocks + j
            own = pl.ds(pl.multiple_of(b * groups, groups), groups)
            lead = banded(wide_filt[own, : 2 * tok], rows)
            back = banded(wide_filt[own, 2 * tok :], rows)
            diag = None
            for a in range(steps):
                now = slice(a * rows, (a + 1) * rows)
                next_rows = slice((steps + a) * rows, (steps + a + 1) * rows)
                span = slice(a * rows, a * rows + 2 * tok)
                keep = keeps[now, :]
                mix = jnp.dot(jnp.concatenate([t * keep for t in lead], axis=0), pwin[span, here], preferred_element_type=F32)
                mix = pick(mix).astype(BF).astype(F32)
                outs[now, here] = (qs[now, here].astype(F32) * mix).astype(BF)
                g_q = (cs[now, here].astype(F32) * mix).astype(BF)
                keep = keeps[next_rows, :]
                grad = jnp.dot(jnp.concatenate([t * keep for t in back], axis=0), gwin[span, here], preferred_element_type=F32)
                grad = pick(grad).astype(BF).astype(F32)
                g_k = (grad * vs[now, here].astype(F32)).astype(BF)
                g_v = (grad * ks[now, here].astype(F32)).astype(BF)
                for p, value in enumerate((g_q, g_k, g_v)):
                    mg[now, part[p]] = value
                    if a == 0:
                        heads[:, part[p]] = value[0:2]
                mine_prod = pwin[tok + a * rows : tok + (a + 1) * rows, here]
                zero = jnp.zeros_like(mine_prod)
                spread = jnp.concatenate([jnp.where(lane_group == g, mine_prod, zero) for g in range(groups)], axis=0)
                pairs = lax.dot_general(spread, gwin[span, here], (((1,), (1,)), ((), ())), preferred_element_type=F32)
                keep = keeps32[next_rows, :]
                pairs = [pairs[g * rows : (g + 1) * rows] * keep for g in range(groups)]
                diag = pairs if diag is None else [s + t for s, t in zip(diag, pairs)]
            sums = jnp.concatenate([diagonal_sums(d, 2 * tok)[:, :tok] for d in diag], axis=0)
            lsum[(b % per_z) // per_x, b // per_z, pl.ds(pl.multiple_of(b % per_x * groups, groups), groups), :] = sums
        begin(row_sends(i))
        out_save(i).start()
        return carry

    lax.fori_loop(0, count, long_step, 0)
    long_one = first_exchange(lsum, l1, 1)
    begin(long_one)
    for i in range(count):
        arrive(row_sends(i))

    pair = slab // ACROSS

    def close_step(i, carry):
        edges = [jnp.concatenate([fore_edge[n]] * (pair // LANES), axis=1) for n in range(3)]
        for j in range(ACROSS):
            here = pl.ds(pl.multiple_of(i * slab + j * pair, LANES), pair)
            g = mg[:, here]
            moved = jnp.dot(fore_shift[...], g, preferred_element_type=F32)
            side = ahead[:, here].astype(F32)
            one, two = moved[:tok], moved[tok:]
            one = jnp.concatenate([one[: tok - 8], one[tok - 8 :] + edges[0] * side[0:1]], axis=0)
            two = jnp.concatenate(
                [two[: tok - 8], two[tok - 8 :] + edges[1] * side[0:1] + edges[2] * side[1:2]], axis=0
            )
            g = g.astype(F32)
            w = w_ref[:, here]
            ys[:, here] = (w[0:1] * g + w[1:2] * one + w[2:3] * two).astype(BF)
            source = xs[:, here].astype(F32)
            ssum[j, i] = jnp.concatenate(
                [jnp.sum(moved_grad * source, axis=0, keepdims=True) for moved_grad in (g, one, two)], axis=0
            )
        y_save(i).start()
        return carry

    half = depth // 2
    lax.fori_loop(0, half, close_step, 0)
    arrive(long_one)
    bl[...] = total(lsum[x], l1, n1)
    long_two = second_exchange(bl, l2, 1)
    begin(long_two)
    lax.fori_loop(half, depth, close_step, 0)
    short_one = first_exchange(ssum, s1, 0)
    begin(short_one)
    arrive(long_two)
    l3[n3] = total(bl[z], l2, n2)
    long_three = third_exchange(l3, 1)
    begin(long_three)
    arrive(short_one)
    bs[...] = total(ssum[x], s1, n1)
    short_two = second_exchange(bs, s2, 0)
    begin(short_two)
    arrive(long_three)
    sums = total(l3[n3], l3, n3) * scales[1]
    l_out[...] = jnp.where(c == 0, sums[: sums.shape[0] // CORES], sums[sums.shape[0] // CORES :])
    arrive(short_two)
    s3[n3] = total(bs[z], s2, n2)
    short_three = third_exchange(s3, 0)
    begin(short_three)
    for i in range(depth):
        y_save(i).wait()
    for i in range(count):
        out_save(i).wait()
        for copy in list(block_sends(i)) + list(row_sends(i)):
            copy.wait_send()
    arrive(short_three)
    sums = total(s3[n3], s3, n3) * scales[0]
    s_out[...] = jnp.where(c == 0, sums[:, : pair // CORES], sums[:, pair // CORES :])
    for copy in long_one + long_two + long_three + short_one + short_two + short_three:
        copy.wait_send()


def local(projected, doc_ids, short_filter, long_filter, cotangent):
    x, cot = projected[0], cotangent[0]
    tok, width = cot.shape
    full = 3 * width
    groups, taps = long_filter.shape
    dps, ctx = lax.axis_size("dp"), lax.axis_size("ctx")
    depth = ctx // (ACROSS * CORES)
    pair = full // (ACROSS * depth)
    some = groups // (ACROSS * depth)
    chunk = 4 * LANES
    n = width // chunk
    n3 = dps * CORES - 1
    links = (ACROSS - 1) + (depth - 1) + n3
    norm = dps * doc_ids.shape[1]
    scales = (1.0 / math.sqrt(norm), 1.0 / math.sqrt(norm * (width // groups)))
    space, far = pl.BlockSpec(memory_space=pltpu.VMEM), pl.BlockSpec(memory_space=pl.ANY)
    dma = pltpu.SemaphoreType.DMA
    half = lambda *s: pltpu.VMEM(s, BF)
    word = lambda *s: pltpu.VMEM(s, F32)
    out, gx, gs, gl = pl.pallas_call(
        functools.partial(whole_kernel, LANES // (width // groups), chunk, depth, scales),
        out_shape=[
            jax.ShapeDtypeStruct((tok, width), BF),
            jax.ShapeDtypeStruct((tok, full), BF),
            jax.ShapeDtypeStruct((3, pair // CORES), F32),
            jax.ShapeDtypeStruct((some // CORES, taps), F32),
        ],
        in_specs=[space] * 3 + [far] * 2,
        out_specs=[far, far, space, space],
        scratch_shapes=[
            half(tok, full), half(tok, width), half(tok, width), half(tok, width), half(tok, width),
            half(3 * tok, width), half(3 * tok, width), half(tok, full), half(tok, full), half(tok, width),
            half(16, full), half(2, full), half(2, full), half(2, full), half(2, full),
            half(2 * tok, tok), half(2 * tok, tok), word(3, 8, LANES), word(3, 8, LANES),
            half(2 * tok, 2 * tok), word(2 * tok, 2 * tok), word(groups, 4 * tok),
            word(ACROSS, depth, 3, pair), word(ACROSS, depth, some, taps),
            word(ACROSS - 1, depth, 3, pair), word(ACROSS - 1, depth, some, taps),
            word(depth - 1, 3, pair), word(depth - 1, some, taps),
            word(n3 + 1, 3, pair), word(n3 + 1, some, taps),
            word(depth, 3, pair), word(depth, some, taps),
            dma, dma((4, n)), dma((n,)), dma((depth,)), dma((2,)), dma((2, n)), dma((2, n)),
            dma((3, n)), dma((3, n)), dma((2, links)), dma((2, links)),
        ],
        compiler_params=pltpu.CompilerParams(collective_id=0, has_side_effects=True, vmem_limit_bytes=VMEM),
        name="whole",
    )(doc_ids, short_filter, long_filter, x, cot)
    return out[None], gx[None], gs, gl


def solution(mesh):
    return jax.shard_map(
        local,
        mesh=mesh,
        in_specs=(P("dp", "ctx", None), P("dp", None), P(), P(), P("dp", "ctx", None)),
        out_specs=(P("dp", "ctx", None), P("dp", "ctx", None), P(None, "ctx"), P("ctx", None)),
        check_vma=False,
    )
```

```python
import functools
import math

import jax
import jax.numpy as jnp
from jax import lax
from jax.experimental import pallas as pl
from jax.experimental.pallas import tpu as pltpu
from jax.sharding import PartitionSpec as P

BF = jnp.bfloat16
F32 = jnp.float32
MESH = pl.DeviceIdType.MESH
ROWS = 16
LANES = 128
CORES = 2
ACROSS = 4
CUTS = 2
VMEM = 56 << 20


def near_docs(doc_ref, tok):
    me = lax.axis_index("ctx")
    last = lax.axis_size("ctx") - 1
    at = lambda i: doc_ref[:, pl.ds(pl.multiple_of(i * tok, tok), tok)]
    before = jnp.where(me > 0, at(jnp.maximum(me - 1, 0)), -1)
    after = jnp.where(me < last, at(jnp.minimum(me + 1, last)), -2)
    return jnp.concatenate([before, at(me), after], axis=1).astype(F32)


def doc_column(row):
    return jnp.broadcast_to(row, (row.shape[1], row.shape[1])).T


def shift_matrix(col, row, steps):
    size = col.shape[0]
    place = lax.broadcasted_iota(jnp.int32, (size, size), 1) - lax.broadcasted_iota(jnp.int32, (size, size), 0)
    return jnp.where((place == steps) & (col == row), 1.0, 0.0).astype(BF)


def ring(steps):
    size = lax.axis_size("ctx")
    return lax.axis_index("dp"), (lax.axis_index("ctx") + size + steps) % size


def sent(src, dst, send, recv, peer):
    return pltpu.make_async_remote_copy(
        src_ref=src, dst_ref=dst, send_sem=send, recv_sem=recv, device_id=peer, device_id_type=MESH
    )


def banded(filt, rows):
    parts = []
    for g in range(filt.shape[0]):
        wide = jnp.broadcast_to(filt[g : g + 1, :], (rows, filt.shape[1]))
        parts.append(pltpu.roll(wide, 0, 1, stride=1, stride_axis=0).astype(BF))
    return parts


def diagonal_sums(part, width):
    half = part.shape[0] // 2
    while half >= 8:
        part = part[:half] + pltpu.roll(part[half:], width - half, 1)
        half //= 2
    while half >= 1:
        part = part + pltpu.roll(pltpu.roll(part, 8 - half, 0), width - half, 1)
        half //= 2
    return part[0:1]


def whole_kernel(groups, chunk, depth, scales, doc_ref, w_ref, filt_ref, x_hbm, cot_hbm, out_hbm, gx_hbm, s_out, l_out,
                 xs, cs, qs, ks, vs, pwin, gwin, mg, ys, outs, tail, mine, border, heads, ahead,
                 back_shift, fore_shift, back_edge, fore_edge, keeps, keeps32, wide_filt, ssum, lsum,
                 s1, l1, s2, l2, s3, l3, bs, bl,
                 tail_sem, in_sem, out_sem, y_sem, edge_sem, blk_send, blk_recv, row_send, row_recv, x_send, x_recv, z_sem, send, recv):
    rows = ROWS
    tok, width = cs.shape
    full = 3 * width
    steps = tok // rows
    count = width // chunk
    blocks = chunk // LANES
    wide = 2 * LANES
    dp, ctx = lax.axis_index("dp"), lax.axis_index("ctx")
    z, x, c = ctx // (ACROSS * CORES), (ctx // CORES) % ACROSS, ctx % CORES
    place = lambda zz, xx, cc: (zz * ACROSS + xx) * CORES + cc
    dps = lax.axis_size("dp")
    across = [(dp, place(z, (x + d) % ACROSS, c)) for d in range(1, ACROSS)]
    along = [(dp, place((z + d) % depth, x, c)) for d in range(1, depth)]
    final = [((dp + d // CORES) % dps, place(z, x, (c + d) % CORES)) for d in range(1, dps * CORES)]
    n1, n2, n3 = len(across), len(along), len(final)
    right, left = ring(1), ring(-1)

    def at(i, size=chunk, offset=0):
        return pl.ds(pl.multiple_of(offset + i * size, LANES), size)

    def loads(i):
        for p in range(3):
            here = at(i, offset=p * width)
            yield pltpu.make_async_copy(x_hbm.at[:, here], xs.at[:, here], in_sem.at[p, i])
        yield pltpu.make_async_copy(cot_hbm.at[:, at(i)], cs.at[:, at(i)], in_sem.at[3, i])

    def block_sends(i):
        own = pl.ds(tok, tok), pl.ds(0, tok)
        yield sent(pwin.at[own[0], at(i)], pwin.at[own[1], at(i)], blk_send.at[0, i], blk_recv.at[0, i], right)
        yield sent(gwin.at[own[1], at(i)], gwin.at[own[0], at(i)], blk_send.at[1, i], blk_recv.at[1, i], left)

    def row_sends(i):
        for p in range(3):
            here = at(i, offset=p * width)
            yield sent(heads.at[:, here], ahead.at[:, here], row_send.at[p, i], row_recv.at[p, i], left)

    def out_save(i):
        return pltpu.make_async_copy(outs.at[:, at(i)], out_hbm.at[:, at(i)], out_sem.at[i])

    slab = full // depth

    def y_save(i):
        here = at((z + 1 + i) % depth, slab)
        return pltpu.make_async_copy(ys.at[:, here], gx_hbm.at[:, here], y_sem.at[i])

    def slab_of(i):
        return (z + 1 + i) % depth

    def x_sends(i):
        to = slab_of(i)
        return [sent(ssum.at[(x + d) % ACROSS, to], s1.at[d - 1, to], x_send.at[d - 1, i], x_recv.at[d - 1, i], across[d - 1])
                for d in range(1, ACROSS)]

    def z_send(i):
        to = slab_of(i)
        return sent(bs.at[to], s2.at[i], z_sem.at[0, i], z_sem.at[1, i], (dp, place(to, x, c)))

    def long_across():
        return [sent(lsum.at[(x + d) % ACROSS], l1.at[d - 1], send.at[1, d - 1], recv.at[1, d - 1], across[d - 1])
                for d in range(1, ACROSS)]

    def long_along():
        return [sent(bl.at[(z + d) % depth], l2.at[d - 1], send.at[1, n1 + d - 1], recv.at[1, n1 + d - 1], along[d - 1])
                for d in range(1, depth)]

    def third_exchange(buf, k):
        return [sent(buf.at[n3], buf.at[d], send.at[k, n1 + n2 + d], recv.at[k, n1 + n2 + d], final[d])
                for d in range(n3)]

    def begin(copies):
        for copy in copies:
            copy.start()

    def arrive(copies):
        for copy in copies:
            copy.wait_recv()

    def total(start, arrived, n):
        for i in range(n):
            start = start + arrived[i]
        return start

    first = pltpu.make_async_copy(x_hbm.at[tok - 16 :, :], tail, tail_sem)
    first.start()
    for i in range(count):
        begin(loads(i))
    peers = [right, left] + across + along + final
    barrier = pltpu.get_barrier_semaphore()
    for peer in peers:
        pl.semaphore_signal(barrier, inc=1, device_id=peer, device_id_type=MESH)
    first.wait()
    mine[...] = tail[14:16, :]
    pl.semaphore_wait(barrier, len(peers))
    edge_copy = sent(mine, border, edge_sem.at[0], edge_sem.at[1], right)
    edge_copy.start()

    docs = near_docs(doc_ref, tok)
    own = docs[:, tok : 2 * tok]
    col = doc_column(own)
    for shifts, sign in ((back_shift, -1), (fore_shift, 1)):
        shifts[0:tok, :] = shift_matrix(col, own, sign)
        shifts[tok:, :] = shift_matrix(col, own, 2 * sign)
    row = lax.broadcasted_iota(jnp.int32, (8, LANES), 0)
    spread_doc = lambda d: jnp.broadcast_to(docs[:, d : d + 1], (8, LANES))
    top, end = col[:8, :], col[tok - 8 :, :]
    old, new = [spread_doc(tok - 1), spread_doc(tok - 2)], [spread_doc(2 * tok), spread_doc(2 * tok + 1)]
    back_edge[0] = jnp.where((row == 0) & (top == old[0]), 1.0, 0.0)
    back_edge[1] = jnp.where((row == 0) & (top == old[1]), 1.0, 0.0)
    back_edge[2] = jnp.where((row == 1) & (top == old[0]), 1.0, 0.0)
    fore_edge[0] = jnp.where((row == 7) & (end == new[0]), 1.0, 0.0)
    fore_edge[1] = jnp.where((row == 6) & (end == new[0]), 1.0, 0.0)
    fore_edge[2] = jnp.where((row == 7) & (end == new[1]), 1.0, 0.0)
    both = jnp.concatenate([col, col], axis=1)
    long_row = jnp.concatenate([jnp.broadcast_to(docs, (8, 3 * tok)), jnp.full((8, tok), -3.0, F32)], axis=1)
    for a in range(steps):
        block_docs = both[a * rows : (a + 1) * rows]
        for b, start in ((a, a * rows), (steps + a, tok + a * rows)):
            window = pltpu.roll(long_row, (4 * tok - start) % (4 * tok), 1)[0:1, : 2 * tok]
            keep = jnp.where(block_docs == window, 1.0, 0.0)
            keeps32[b * rows : (b + 1) * rows, :] = keep
            keeps[b * rows : (b + 1) * rows, :] = keep.astype(BF)
    pwin[2 * tok :, :] = jnp.zeros((tok, width), BF)
    gwin[2 * tok :, :] = jnp.zeros((tok, width), BF)
    filt = filt_ref[...]
    turn = lax.broadcasted_iota(jnp.int32, (tok, tok), 0) + lax.broadcasted_iota(jnp.int32, (tok, tok), 1)
    wide_filt[:, 0:tok] = jnp.dot(filt, jnp.where(turn == tok, 1.0, 0.0).astype(BF), preferred_element_type=F32)
    filt = filt.astype(F32)
    lane = lax.broadcasted_iota(jnp.int32, filt.shape, 1)
    wide_filt[:, tok : 2 * tok] = jnp.where(lane == 0, filt, 0.0)
    wide_filt[:, 2 * tok : 3 * tok] = filt
    wide_filt[:, 3 * tok :] = jnp.zeros(filt.shape, F32)
    edge_copy.wait()

    def mixed(i, j, part):
        here = pl.ds(pl.multiple_of(part * width + i * chunk + j * wide, LANES), wide)
        edges = [jnp.concatenate([back_edge[n]] * 2, axis=1) for n in range(3)]
        value = xs[:, here]
        moved = jnp.dot(back_shift[...], value, preferred_element_type=F32)
        side = border[:, here].astype(F32)
        w = w_ref[:, here]
        mix = w[0:1] * value.astype(F32) + w[1:2] * moved[:tok] + w[2:3] * moved[tok:]
        fix = w[1:2] * (edges[0] * side[1:2]) + w[2:3] * (edges[1] * side[0:1] + edges[2] * side[1:2])
        return jnp.concatenate([mix[:8] + fix, mix[8:]], axis=0).astype(BF)

    def mix_step(i, carry):
        for copy in loads(i):
            copy.wait()
        for j in range(chunk // wide):
            here = pl.ds(pl.multiple_of(i * chunk + j * wide, LANES), wide)
            q, k, v = mixed(i, j, 0), mixed(i, j, 1), mixed(i, j, 2)
            qs[:, here], ks[:, here], vs[:, here] = q, k, v
            gwin[0:tok, here] = (cs[:, here].astype(F32) * q.astype(F32)).astype(BF)
            pwin[tok : 2 * tok, here] = (k.astype(F32) * v.astype(F32)).astype(BF)
        begin(block_sends(i))
        return carry

    lax.fori_loop(0, count, mix_step, 0)

    lane_group = lax.broadcasted_iota(jnp.int32, (rows, LANES), 1) // (LANES // groups)

    def pick(value):
        chosen = value[:rows]
        for g in range(1, groups):
            chosen = jnp.where(lane_group == g, value[g * rows : (g + 1) * rows], chosen)
        return chosen

    per_z = count * blocks // depth
    per_x = per_z // ACROSS

    def long_step(i, carry):
        arrive(block_sends(i))
        for j in range(blocks):
            part = [pl.ds(pl.multiple_of(p * width + i * chunk + j * LANES, LANES), LANES) for p in range(3)]
            here = part[0]
            b = i * blocks + j
            own = pl.ds(pl.multiple_of(b * groups, groups), groups)
            lead = banded(wide_filt[own, : 2 * tok], rows)
            back = banded(wide_filt[own, 2 * tok :], rows)
            diag = None
            for a in range(steps):
                now = slice(a * rows, (a + 1) * rows)
                next_rows = slice((steps + a) * rows, (steps + a + 1) * rows)
                span = slice(a * rows, a * rows + 2 * tok)
                keep = keeps[now, :]
                mix = jnp.dot(jnp.concatenate([t * keep for t in lead], axis=0), pwin[span, here], preferred_element_type=F32)
                mix = pick(mix).astype(BF).astype(F32)
                outs[now, here] = (qs[now, here].astype(F32) * mix).astype(BF)
                g_q = (cs[now, here].astype(F32) * mix).astype(BF)
                keep = keeps[next_rows, :]
                grad = jnp.dot(jnp.concatenate([t * keep for t in back], axis=0), gwin[span, here], preferred_element_type=F32)
                grad = pick(grad).astype(BF).astype(F32)
                g_k = (grad * vs[now, here].astype(F32)).astype(BF)
                g_v = (grad * ks[now, here].astype(F32)).astype(BF)
                for p, value in enumerate((g_q, g_k, g_v)):
                    mg[now, part[p]] = value
                    if a == 0:
                        heads[:, part[p]] = value[0:2]
                mine_prod = pwin[tok + a * rows : tok + (a + 1) * rows, here]
                zero = jnp.zeros_like(mine_prod)
                spread = jnp.concatenate([jnp.where(lane_group == g, mine_prod, zero) for g in range(groups)], axis=0)
                pairs = lax.dot_general(spread, gwin[span, here], (((1,), (1,)), ((), ())), preferred_element_type=F32)
                keep = keeps32[next_rows, :]
                pairs = [pairs[g * rows : (g + 1) * rows] * keep for g in range(groups)]
                diag = pairs if diag is None else [s + t for s, t in zip(diag, pairs)]
            sums = jnp.concatenate([diagonal_sums(d, 2 * tok)[:, :tok] for d in diag], axis=0)
            lsum[(b % per_z) // per_x, b // per_z, pl.ds(pl.multiple_of(b % per_x * groups, groups), groups), :] = sums
        begin(row_sends(i))
        out_save(i).start()
        return carry

    lax.fori_loop(0, count, long_step, 0)
    long_one = long_across()
    begin(long_one)
    for i in range(count):
        arrive(row_sends(i))

    pair = slab // ACROSS

    def close_slab(i):
        to = slab_of(i)
        edges = [jnp.concatenate([fore_edge[n]] * (pair // LANES), axis=1) for n in range(3)]
        for j in range(ACROSS):
            here = pl.ds(pl.multiple_of(to * slab + j * pair, LANES), pair)
            g = mg[:, here]
            moved = jnp.dot(fore_shift[...], g, preferred_element_type=F32)
            side = ahead[:, here].astype(F32)
            one, two = moved[:tok], moved[tok:]
            one = jnp.concatenate([one[: tok - 8], one[tok - 8 :] + edges[0] * side[0:1]], axis=0)
            two = jnp.concatenate(
                [two[: tok - 8], two[tok - 8 :] + edges[1] * side[0:1] + edges[2] * side[1:2]], axis=0
            )
            g = g.astype(F32)
            w = w_ref[:, here]
            ys[:, here] = (w[0:1] * g + w[1:2] * one + w[2:3] * two).astype(BF)
            source = xs[:, here].astype(F32)
            ssum[j, to] = jnp.concatenate(
                [jnp.sum(moved_grad * source, axis=0, keepdims=True) for moved_grad in (g, one, two)], axis=0
            )
        begin(x_sends(i))
        y_save(i).start()

    def pass_on(i):
        arrive(x_sends(i))
        to = slab_of(i)
        bs[to] = total(ssum[x, to], [s1[d, to] for d in range(n1)], n1)

    def close_step(i, carry):
        close_slab(i)
        return carry

    half = depth // 2
    lax.fori_loop(0, half, close_step, 0)
    arrive(long_one)
    bl[...] = total(lsum[x], l1, n1)
    long_two = long_along()
    begin(long_two)
    lax.fori_loop(half, depth, close_step, 0)
    for i in range(n2):
        pass_on(i)
        z_send(i).start()
    arrive(long_two)
    l3[n3] = total(bl[z], l2, n2)
    long_three = third_exchange(l3, 1)
    begin(long_three)
    pass_on(depth - 1)
    for i in range(n2):
        z_send(i).wait_recv()
    s3[n3] = total(bs[z], s2, n2)
    short_three = third_exchange(s3, 0)
    begin(short_three)
    arrive(long_three)
    sums = total(l3[n3], l3, n3) * scales[1]
    l_out[...] = jnp.where(c == 0, sums[: sums.shape[0] // CORES], sums[sums.shape[0] // CORES :])
    for i in range(depth):
        y_save(i).wait()
        for copy in x_sends(i):
            copy.wait_send()
    for i in range(n2):
        z_send(i).wait_send()
    for i in range(count):
        out_save(i).wait()
        for copy in list(block_sends(i)) + list(row_sends(i)):
            copy.wait_send()
    for copy in long_one + long_two + long_three:
        copy.wait_send()
    arrive(short_three)
    sums = total(s3[n3], s3, n3) * scales[0]
    s_out[...] = jnp.where(c == 0, sums[:, : pair // CORES], sums[:, pair // CORES :])
    for copy in short_three:
        copy.wait_send()


def copy_kernel(*refs):
    count = len(refs) // 2
    for src, dst in zip(refs[:count], refs[count:]):
        dst[...] = src[...]


def copied(large, small, cuts):
    def spec(a):
        return pl.BlockSpec((a.shape[0] // cuts, a.shape[1]), lambda i: (i, 0))

    specs = [spec(a) for a in large] + [pl.BlockSpec(a.shape, lambda i: (0, 0)) for a in small]
    return pl.pallas_call(
        copy_kernel,
        grid=(cuts,),
        out_shape=[jax.ShapeDtypeStruct(a.shape, a.dtype) for a in large + small],
        in_specs=specs,
        out_specs=specs,
        compiler_params=pltpu.CompilerParams(vmem_limit_bytes=VMEM),
        name="place",
    )(*large, *small)


def local(projected, doc_ids, short_filter, long_filter, cotangent):
    x, cot = projected[0], cotangent[0]
    tok, width = cot.shape
    full = 3 * width
    groups, taps = long_filter.shape
    dps, ctx = lax.axis_size("dp"), lax.axis_size("ctx")
    depth = ctx // (ACROSS * CORES)
    pair = full // (ACROSS * depth)
    some = groups // (ACROSS * depth)
    chunk = 4 * LANES
    n = width // chunk
    n3 = dps * CORES - 1
    links = (ACROSS - 1) + (depth - 1) + n3
    norm = dps * doc_ids.shape[1]
    scales = (1.0 / math.sqrt(norm), 1.0 / math.sqrt(norm * (width // groups)))
    space, far = pl.BlockSpec(memory_space=pltpu.VMEM), pl.BlockSpec(memory_space=pl.ANY)
    dma = pltpu.SemaphoreType.DMA
    half = lambda *s: pltpu.VMEM(s, BF)
    word = lambda *s: pltpu.VMEM(s, F32)
    out, gx, gs, gl = pl.pallas_call(
        functools.partial(whole_kernel, LANES // (width // groups), chunk, depth, scales),
        out_shape=[
            jax.ShapeDtypeStruct((tok, width), BF),
            jax.ShapeDtypeStruct((tok, full), BF),
            jax.ShapeDtypeStruct((3, pair // CORES), F32),
            jax.ShapeDtypeStruct((some // CORES, taps), F32),
        ],
        in_specs=[space] * 3 + [far] * 2,
        out_specs=[far, far, space, space],
        scratch_shapes=[
            half(tok, full), half(tok, width), half(tok, width), half(tok, width), half(tok, width),
            half(3 * tok, width), half(3 * tok, width), half(tok, full), half(tok, full), half(tok, width),
            half(16, full), half(2, full), half(2, full), half(2, full), half(2, full),
            half(2 * tok, tok), half(2 * tok, tok), word(3, 8, LANES), word(3, 8, LANES),
            half(2 * tok, 2 * tok), word(2 * tok, 2 * tok), word(groups, 4 * tok),
            word(ACROSS, depth, 3, pair), word(ACROSS, depth, some, taps),
            word(ACROSS - 1, depth, 3, pair), word(ACROSS - 1, depth, some, taps),
            word(depth - 1, 3, pair), word(depth - 1, some, taps),
            word(n3 + 1, 3, pair), word(n3 + 1, some, taps),
            word(depth, 3, pair), word(depth, some, taps),
            dma, dma((4, n)), dma((n,)), dma((depth,)), dma((2,)), dma((2, n)), dma((2, n)),
            dma((3, n)), dma((3, n)), dma((ACROSS - 1, depth)), dma((ACROSS - 1, depth)), dma((2, depth)),
            dma((2, links)), dma((2, links)),
        ],
        compiler_params=pltpu.CompilerParams(collective_id=0, has_side_effects=True, vmem_limit_bytes=VMEM),
        name="whole",
    )(doc_ids, short_filter, long_filter, x, cot)
    out, gx, gs, gl = copied([out, gx], [gs, gl], CUTS)
    return out[None], gx[None], gs, gl


def solution(mesh):
    return jax.shard_map(
        local,
        mesh=mesh,
        in_specs=(P("dp", "ctx", None), P("dp", None), P(), P(), P("dp", "ctx", None)),
        out_specs=(P("dp", "ctx", None), P("dp", "ctx", None), P(None, "ctx"), P("ctx", None)),
        check_vma=False,
    )
```

```python
import functools
import math

import jax
import jax.numpy as jnp
from jax import lax
from jax.experimental import pallas as pl
from jax.experimental.pallas import tpu as pltpu
from jax.sharding import PartitionSpec as P

BF = jnp.bfloat16
F32 = jnp.float32
MESH = pl.DeviceIdType.MESH
ROWS = 16
LANES = 128
CORES = 2
ACROSS = 4
CUTS = 2
VMEM = 32 << 20


def near_docs(doc_ref, tok):
    me = lax.axis_index("ctx")
    last = lax.axis_size("ctx") - 1
    at = lambda i: doc_ref[:, pl.ds(pl.multiple_of(i * tok, tok), tok)]
    before = jnp.where(me > 0, at(jnp.maximum(me - 1, 0)), -1)
    after = jnp.where(me < last, at(jnp.minimum(me + 1, last)), -2)
    return jnp.concatenate([before, at(me), after], axis=1).astype(F32)


def doc_column(row):
    return jnp.broadcast_to(row, (row.shape[1], row.shape[1])).T


def shift_matrix(col, row, steps):
    size = col.shape[0]
    place = lax.broadcasted_iota(jnp.int32, (size, size), 1) - lax.broadcasted_iota(jnp.int32, (size, size), 0)
    return jnp.where((place == steps) & (col == row), 1.0, 0.0).astype(BF)


def ring(steps):
    size = lax.axis_size("ctx")
    return lax.axis_index("dp"), (lax.axis_index("ctx") + size + steps) % size


def sent(src, dst, send, recv, peer):
    return pltpu.make_async_remote_copy(
        src_ref=src, dst_ref=dst, send_sem=send, recv_sem=recv, device_id=peer, device_id_type=MESH
    )


def banded(filt, rows):
    parts = []
    for g in range(filt.shape[0]):
        wide = jnp.broadcast_to(filt[g : g + 1, :], (rows, filt.shape[1]))
        parts.append(pltpu.roll(wide, 0, 1, stride=1, stride_axis=0).astype(BF))
    return parts


def diagonal_sums(part, width):
    half = part.shape[0] // 2
    while half >= 8:
        part = part[:half] + pltpu.roll(part[half:], width - half, 1)
        half //= 2
    while half >= 1:
        part = part + pltpu.roll(pltpu.roll(part, 8 - half, 0), width - half, 1)
        half //= 2
    return part[0:1]


def whole_kernel(groups, chunk, depth, scales, doc_hbm, w_hbm, filt_hbm, x_hbm, cot_hbm, out_hbm, gx_hbm, s_out, l_out,
                 doc_ref, w_ref, filt_ref, table_sem, xs, cs, qs, ks, vs, pwin, gwin, mg, ys, outs, tail, mine, border, heads, ahead,
                 back_shift, fore_shift, back_edge, fore_edge, keeps, keeps32, wide_filt, ssum, lsum,
                 s1, l1, s2, l2, s3, l3, bs, bl,
                 tail_sem, in_sem, out_sem, y_sem, edge_sem, blk_send, blk_recv, row_send, row_recv, x_send, x_recv, z_sem, send, recv):
    rows = ROWS
    tok, width = cs.shape
    full = 3 * width
    steps = tok // rows
    count = width // chunk
    blocks = chunk // LANES
    wide = 2 * LANES
    dp, ctx = lax.axis_index("dp"), lax.axis_index("ctx")
    z, x, c = ctx // (ACROSS * CORES), (ctx // CORES) % ACROSS, ctx % CORES
    place = lambda zz, xx, cc: (zz * ACROSS + xx) * CORES + cc
    dps = lax.axis_size("dp")
    across = [(dp, place(z, (x + d) % ACROSS, c)) for d in range(1, ACROSS)]
    along = [(dp, place((z + d) % depth, x, c)) for d in range(1, depth)]
    final = [((dp + d // CORES) % dps, place(z, x, (c + d) % CORES)) for d in range(1, dps * CORES)]
    n1, n2, n3 = len(across), len(along), len(final)
    right, left = ring(1), ring(-1)

    def at(i, size=chunk, offset=0):
        return pl.ds(pl.multiple_of(offset + i * size, LANES), size)

    def loads(i):
        for p in range(3):
            here = at(i, offset=p * width)
            yield pltpu.make_async_copy(x_hbm.at[:, here], xs.at[:, here], in_sem.at[p, i])
        yield pltpu.make_async_copy(cot_hbm.at[:, at(i)], cs.at[:, at(i)], in_sem.at[3, i])

    def block_sends(i):
        own = pl.ds(tok, tok), pl.ds(0, tok)
        yield sent(pwin.at[own[0], at(i)], pwin.at[own[1], at(i)], blk_send.at[0, i], blk_recv.at[0, i], right)
        yield sent(gwin.at[own[1], at(i)], gwin.at[own[0], at(i)], blk_send.at[1, i], blk_recv.at[1, i], left)

    def row_sends(i):
        for p in range(3):
            here = at(i, offset=p * width)
            yield sent(heads.at[:, here], ahead.at[:, here], row_send.at[p, i], row_recv.at[p, i], left)

    def out_save(i):
        return pltpu.make_async_copy(outs.at[:, at(i)], out_hbm.at[:, at(i)], out_sem.at[i])

    slab = full // depth

    def y_save(i):
        here = at((z + 1 + i) % depth, slab)
        return pltpu.make_async_copy(ys.at[:, here], gx_hbm.at[:, here], y_sem.at[i])

    def slab_of(i):
        return (z + 1 + i) % depth

    def x_sends(i):
        to = slab_of(i)
        return [sent(ssum.at[(x + d) % ACROSS, to], s1.at[d - 1, to], x_send.at[d - 1, i], x_recv.at[d - 1, i], across[d - 1])
                for d in range(1, ACROSS)]

    def z_send(i):
        to = slab_of(i)
        return sent(bs.at[to], s2.at[i], z_sem.at[0, i], z_sem.at[1, i], (dp, place(to, x, c)))

    def long_across():
        return [sent(lsum.at[(x + d) % ACROSS], l1.at[d - 1], send.at[1, d - 1], recv.at[1, d - 1], across[d - 1])
                for d in range(1, ACROSS)]

    def long_along():
        return [sent(bl.at[(z + d) % depth], l2.at[d - 1], send.at[1, n1 + d - 1], recv.at[1, n1 + d - 1], along[d - 1])
                for d in range(1, depth)]

    def third_exchange(buf, k):
        return [sent(buf.at[n3], buf.at[d], send.at[k, n1 + n2 + d], recv.at[k, n1 + n2 + d], final[d])
                for d in range(n3)]

    def begin(copies):
        for copy in copies:
            copy.start()

    def arrive(copies):
        for copy in copies:
            copy.wait_recv()

    def total(start, arrived, n):
        for i in range(n):
            start = start + arrived[i]
        return start

    first = pltpu.make_async_copy(x_hbm.at[tok - 16 :, :], tail, tail_sem)
    first.start()
    pairs = ((doc_hbm, doc_ref), (filt_hbm, filt_ref), (w_hbm, w_ref))
    tables = [pltpu.make_async_copy(src, dst, table_sem.at[n]) for n, (src, dst) in enumerate(pairs)]
    begin(tables)
    for i in range(count):
        begin(loads(i))
    peers = [right, left] + across + along + final
    barrier = pltpu.get_barrier_semaphore()
    for peer in peers:
        pl.semaphore_signal(barrier, inc=1, device_id=peer, device_id_type=MESH)
    first.wait()
    mine[...] = tail[14:16, :]
    pl.semaphore_wait(barrier, len(peers))
    edge_copy = sent(mine, border, edge_sem.at[0], edge_sem.at[1], right)
    edge_copy.start()

    for copy in tables:
        copy.wait()
    docs = near_docs(doc_ref, tok)
    own = docs[:, tok : 2 * tok]
    col = doc_column(own)
    for shifts, sign in ((back_shift, -1), (fore_shift, 1)):
        shifts[0:tok, :] = shift_matrix(col, own, sign)
        shifts[tok:, :] = shift_matrix(col, own, 2 * sign)
    row = lax.broadcasted_iota(jnp.int32, (8, LANES), 0)
    spread_doc = lambda d: jnp.broadcast_to(docs[:, d : d + 1], (8, LANES))
    end = col[tok - 8 :, :]
    new = [spread_doc(2 * tok), spread_doc(2 * tok + 1)]
    past = jnp.concatenate([docs, jnp.full((1, tok), -3.0, F32)], axis=1)
    for n in range(2):
        earlier = pltpu.roll(jnp.broadcast_to(past, (8, 4 * tok)), n + 1, 1)[0:1, tok : 2 * tok]
        back_edge[n] = jnp.where(col[:16, :] == doc_column(earlier)[:16, :], 1.0, 0.0)
    fore_edge[0] = jnp.where((row == 7) & (end == new[0]), 1.0, 0.0)
    fore_edge[1] = jnp.where((row == 6) & (end == new[0]), 1.0, 0.0)
    fore_edge[2] = jnp.where((row == 7) & (end == new[1]), 1.0, 0.0)
    both = jnp.concatenate([col, col], axis=1)
    long_row = jnp.concatenate([jnp.broadcast_to(docs, (8, 3 * tok)), jnp.full((8, tok), -3.0, F32)], axis=1)
    for a in range(steps):
        block_docs = both[a * rows : (a + 1) * rows]
        for b, start in ((a, a * rows), (steps + a, tok + a * rows)):
            window = pltpu.roll(long_row, (4 * tok - start) % (4 * tok), 1)[0:1, : 2 * tok]
            keep = jnp.where(block_docs == window, 1.0, 0.0)
            keeps32[b * rows : (b + 1) * rows, :] = keep
            keeps[b * rows : (b + 1) * rows, :] = keep.astype(BF)
    pwin[2 * tok :, :] = jnp.zeros((tok, width), BF)
    gwin[2 * tok :, :] = jnp.zeros((tok, width), BF)
    filt = filt_ref[...]
    turn = lax.broadcasted_iota(jnp.int32, (tok, tok), 0) + lax.broadcasted_iota(jnp.int32, (tok, tok), 1)
    wide_filt[:, 0:tok] = jnp.dot(filt, jnp.where(turn == tok, 1.0, 0.0).astype(BF), preferred_element_type=F32)
    filt = filt.astype(F32)
    lane = lax.broadcasted_iota(jnp.int32, filt.shape, 1)
    wide_filt[:, tok : 2 * tok] = jnp.where(lane == 0, filt, 0.0)
    wide_filt[:, 2 * tok : 3 * tok] = filt
    wide_filt[:, 3 * tok :] = jnp.zeros(filt.shape, F32)
    def mixed(i, j, part):
        here = pl.ds(pl.multiple_of(part * width + i * chunk + j * wide, LANES), wide)
        value = xs[:, here]
        moved = jnp.dot(back_shift[...], value, preferred_element_type=F32)
        w = w_ref[:, here]
        return (w[0:1] * value.astype(F32) + w[1:2] * moved[:tok] + w[2:3] * moved[tok:]).astype(BF)

    def mix_step(i, carry):
        for copy in loads(i):
            copy.wait()
        for j in range(chunk // wide):
            here = pl.ds(pl.multiple_of(i * chunk + j * wide, LANES), wide)
            q, k, v = mixed(i, j, 0), mixed(i, j, 1), mixed(i, j, 2)
            qs[:, here], ks[:, here], vs[:, here] = q, k, v
            gwin[0:tok, here] = (cs[:, here].astype(F32) * q.astype(F32)).astype(BF)
            pwin[tok : 2 * tok, here] = (k.astype(F32) * v.astype(F32)).astype(BF)
        return carry

    def top_rows(i, part):
        here = at(i, offset=part * width)
        place_row = lax.broadcasted_iota(jnp.int32, (16, chunk), 0)
        keep = [jnp.concatenate([back_edge[n]] * (chunk // LANES), axis=1) for n in range(2)]
        value = xs[0:16, here].astype(F32)
        side = border[:, here].astype(F32)
        one = jnp.where(place_row == 0, side[1:2], pltpu.roll(value, 1, 0))
        two = jnp.where(place_row == 0, side[0:1], jnp.where(place_row == 1, side[1:2], pltpu.roll(value, 2, 0)))
        w = w_ref[:, here]
        return (w[0:1] * value + w[1:2] * (keep[0] * one) + w[2:3] * (keep[1] * two)).astype(BF)

    def fix_step(i, carry):
        here = at(i)
        q, k, v = top_rows(i, 0), top_rows(i, 1), top_rows(i, 2)
        qs[0:16, here], ks[0:16, here], vs[0:16, here] = q, k, v
        gwin[0:16, here] = (cs[0:16, here].astype(F32) * q.astype(F32)).astype(BF)
        pwin[tok : tok + 16, here] = (k.astype(F32) * v.astype(F32)).astype(BF)
        return carry

    middle, ready = count // 2, count
    lax.fori_loop(0, middle, mix_step, 0)
    edge_copy.wait()
    for i in range(middle):
        fix_step(i, 0)
        begin(block_sends(i))
    lax.fori_loop(middle, count, mix_step, 0)
    for i in range(middle, count):
        fix_step(i, 0)
        begin(block_sends(i))

    lane_group = lax.broadcasted_iota(jnp.int32, (rows, LANES), 1) // (LANES // groups)

    def pick(value):
        chosen = value[:rows]
        for g in range(1, groups):
            chosen = jnp.where(lane_group == g, value[g * rows : (g + 1) * rows], chosen)
        return chosen

    per_z = count * blocks // depth
    per_x = per_z // ACROSS

    def long_step(i, carry):
        @pl.when(i + ready < count)
        def _():
            begin(block_sends(i + ready))

        arrive(block_sends(i))
        for j in range(blocks):
            part = [pl.ds(pl.multiple_of(p * width + i * chunk + j * LANES, LANES), LANES) for p in range(3)]
            here = part[0]
            b = i * blocks + j
            own = pl.ds(pl.multiple_of(b * groups, groups), groups)
            lead = banded(wide_filt[own, : 2 * tok], rows)
            back = banded(wide_filt[own, 2 * tok :], rows)
            diag = None
            for a in range(steps):
                now = slice(a * rows, (a + 1) * rows)
                next_rows = slice((steps + a) * rows, (steps + a + 1) * rows)
                span = slice(a * rows, a * rows + 2 * tok)
                keep = keeps[now, :]
                mix = jnp.dot(jnp.concatenate([t * keep for t in lead], axis=0), pwin[span, here], preferred_element_type=F32)
                mix = pick(mix).astype(BF).astype(F32)
                outs[now, here] = (qs[now, here].astype(F32) * mix).astype(BF)
                g_q = (cs[now, here].astype(F32) * mix).astype(BF)
                keep = keeps[next_rows, :]
                grad = jnp.dot(jnp.concatenate([t * keep for t in back], axis=0), gwin[span, here], preferred_element_type=F32)
                grad = pick(grad).astype(BF).astype(F32)
                g_k = (grad * vs[now, here].astype(F32)).astype(BF)
                g_v = (grad * ks[now, here].astype(F32)).astype(BF)
                for p, value in enumerate((g_q, g_k, g_v)):
                    mg[now, part[p]] = value
                    if a == 0:
                        heads[:, part[p]] = value[0:2]
                mine_prod = pwin[tok + a * rows : tok + (a + 1) * rows, here]
                zero = jnp.zeros_like(mine_prod)
                spread = jnp.concatenate([jnp.where(lane_group == g, mine_prod, zero) for g in range(groups)], axis=0)
                pairs = lax.dot_general(spread, gwin[span, here], (((1,), (1,)), ((), ())), preferred_element_type=F32)
                keep = keeps32[next_rows, :]
                pairs = [pairs[g * rows : (g + 1) * rows] * keep for g in range(groups)]
                diag = pairs if diag is None else [s + t for s, t in zip(diag, pairs)]
            sums = jnp.concatenate([diagonal_sums(d, 2 * tok)[:, :tok] for d in diag], axis=0)
            lsum[(b % per_z) // per_x, b // per_z, pl.ds(pl.multiple_of(b % per_x * groups, groups), groups), :] = sums
        begin(row_sends(i))
        out_save(i).start()
        return carry

    lax.fori_loop(0, count, long_step, 0)
    long_one = long_across()
    begin(long_one)
    for i in range(count):
        arrive(row_sends(i))

    pair = slab // ACROSS

    def close_slab(i):
        to = slab_of(i)
        edges = [jnp.concatenate([fore_edge[n]] * (pair // LANES), axis=1) for n in range(3)]
        for j in range(ACROSS):
            here = pl.ds(pl.multiple_of(to * slab + j * pair, LANES), pair)
            g = mg[:, here]
            moved = jnp.dot(fore_shift[...], g, preferred_element_type=F32)
            side = ahead[:, here].astype(F32)
            one, two = moved[:tok], moved[tok:]
            one = jnp.concatenate([one[: tok - 8], one[tok - 8 :] + edges[0] * side[0:1]], axis=0)
            two = jnp.concatenate(
                [two[: tok - 8], two[tok - 8 :] + edges[1] * side[0:1] + edges[2] * side[1:2]], axis=0
            )
            g = g.astype(F32)
            w = w_ref[:, here]
            ys[:, here] = (w[0:1] * g + w[1:2] * one + w[2:3] * two).astype(BF)
            source = xs[:, here].astype(F32)
            ssum[j, to] = jnp.concatenate(
                [jnp.sum(moved_grad * source, axis=0, keepdims=True) for moved_grad in (g, one, two)], axis=0
            )
        begin(x_sends(i))
        y_save(i).start()

    def pass_on(i):
        arrive(x_sends(i))
        to = slab_of(i)
        bs[to] = total(ssum[x, to], [s1[d, to] for d in range(n1)], n1)

    def close_step(i, carry):
        close_slab(i)
        return carry

    half = depth // 2
    lax.fori_loop(0, half, close_step, 0)
    arrive(long_one)
    bl[...] = total(lsum[x], l1, n1)
    long_two = long_along()
    begin(long_two)
    lax.fori_loop(half, depth, close_step, 0)
    for i in range(n2):
        pass_on(i)
        z_send(i).start()
    arrive(long_two)
    l3[n3] = total(bl[z], l2, n2)
    long_three = third_exchange(l3, 1)
    begin(long_three)
    pass_on(depth - 1)
    for i in range(n2):
        z_send(i).wait_recv()
    s3[n3] = total(bs[z], s2, n2)
    short_three = third_exchange(s3, 0)
    begin(short_three)
    arrive(long_three)
    sums = total(l3[n3], l3, n3) * scales[1]
    l_out[...] = jnp.where(c == 0, sums[: sums.shape[0] // CORES], sums[sums.shape[0] // CORES :])
    for i in range(depth):
        y_save(i).wait()
        for copy in x_sends(i):
            copy.wait_send()
    for i in range(n2):
        z_send(i).wait_send()
    for i in range(count):
        out_save(i).wait()
        for copy in list(block_sends(i)) + list(row_sends(i)):
            copy.wait_send()
    for copy in long_one + long_two + long_three:
        copy.wait_send()
    arrive(short_three)
    sums = total(s3[n3], s3, n3) * scales[0]
    s_out[...] = jnp.where(c == 0, sums[:, : pair // CORES], sums[:, pair // CORES :])
    for copy in short_three:
        copy.wait_send()


def copy_kernel(*refs):
    count = len(refs) // 2
    for src, dst in zip(refs[:count], refs[count:]):
        dst[...] = src[...]


def copied(large, small, cuts):
    def spec(a):
        return pl.BlockSpec((a.shape[0] // cuts, a.shape[1]), lambda i: (i, 0))

    specs = [spec(a) for a in large] + [pl.BlockSpec(a.shape, lambda i: (0, 0)) for a in small]
    return pl.pallas_call(
        copy_kernel,
        grid=(cuts,),
        out_shape=[jax.ShapeDtypeStruct(a.shape, a.dtype) for a in large + small],
        in_specs=specs,
        out_specs=specs,
        compiler_params=pltpu.CompilerParams(vmem_limit_bytes=VMEM),
        name="place",
    )(*large, *small)


def local(projected, doc_ids, short_filter, long_filter, cotangent):
    x, cot = projected[0], cotangent[0]
    tok, width = cot.shape
    full = 3 * width
    groups, taps = long_filter.shape
    dps, ctx = lax.axis_size("dp"), lax.axis_size("ctx")
    depth = ctx // (ACROSS * CORES)
    pair = full // (ACROSS * depth)
    some = groups // (ACROSS * depth)
    chunk = 4 * LANES
    n = width // chunk
    n3 = dps * CORES - 1
    links = (ACROSS - 1) + (depth - 1) + n3
    norm = dps * doc_ids.shape[1]
    scales = (1.0 / math.sqrt(norm), 1.0 / math.sqrt(norm * (width // groups)))
    space, far = pl.BlockSpec(memory_space=pltpu.VMEM), pl.BlockSpec(memory_space=pl.ANY)
    dma = pltpu.SemaphoreType.DMA
    half = lambda *s: pltpu.VMEM(s, BF)
    word = lambda *s: pltpu.VMEM(s, F32)
    doc_ids, short_filter, long_filter, x, cot = [pltpu.with_memory_space_constraint(a, pltpu.HBM) for a in (doc_ids, short_filter, long_filter, x, cot)]
    out, gx, gs, gl = pl.pallas_call(
        functools.partial(whole_kernel, LANES // (width // groups), chunk, depth, scales),
        out_shape=[
            jax.ShapeDtypeStruct((tok, width), BF),
            jax.ShapeDtypeStruct((tok, full), BF),
            jax.ShapeDtypeStruct((3, pair // CORES), F32),
            jax.ShapeDtypeStruct((some // CORES, taps), F32),
        ],
        in_specs=[pl.BlockSpec(memory_space=pltpu.HBM)] * 5,
        out_specs=[far, far, space, space],
        scratch_shapes=[
            pltpu.VMEM(doc_ids.shape, jnp.int32), word(3, full), half(groups, taps), dma((3,)),
            half(tok, full), half(tok, width), half(tok, width), half(tok, width), half(tok, width),
            half(3 * tok, width), half(3 * tok, width), half(tok, full), half(tok, full), half(tok, width),
            half(16, full), half(2, full), half(2, full), half(2, full), half(2, full),
            half(2 * tok, tok), half(2 * tok, tok), word(2, 16, LANES), word(3, 8, LANES),
            half(2 * tok, 2 * tok), word(2 * tok, 2 * tok), word(groups, 4 * tok),
            word(ACROSS, depth, 3, pair), word(ACROSS, depth, some, taps),
            word(ACROSS - 1, depth, 3, pair), word(ACROSS - 1, depth, some, taps),
            word(depth - 1, 3, pair), word(depth - 1, some, taps),
            word(n3 + 1, 3, pair), word(n3 + 1, some, taps),
            word(depth, 3, pair), word(depth, some, taps),
            dma, dma((4, n)), dma((n,)), dma((depth,)), dma((2,)), dma((2, n)), dma((2, n)),
            dma((3, n)), dma((3, n)), dma((ACROSS - 1, depth)), dma((ACROSS - 1, depth)), dma((2, depth)),
            dma((2, links)), dma((2, links)),
        ],
        compiler_params=pltpu.CompilerParams(collective_id=0, has_side_effects=True, vmem_limit_bytes=VMEM),
        name="whole",
    )(doc_ids, short_filter, long_filter, x, cot)
    out, gx, gs, gl = copied([out, gx], [gs, gl], CUTS)
    return out[None], gx[None], gs, gl


def solution(mesh):
    return jax.shard_map(
        local,
        mesh=mesh,
        in_specs=(P("dp", "ctx", None), P("dp", None), P(), P(), P("dp", "ctx", None)),
        out_specs=(P("dp", "ctx", None), P("dp", "ctx", None), P(None, "ctx"), P("ctx", None)),
        check_vma=False,
    )
```
